128 devices in a mesh: face: 8 (over y, core), tile: 16 (over z, x).
Axes of the slice: x: 4, y: 4, z: 4, core: 2. Of those that a mesh axis runs over, the one named last changes fastest.
Arguments:
- met_src: bfloat16 [8192, 48, 128], P(('face', 'tile')), may hold values from -6 to 6
- intersection_weights: bfloat16 [8192, 128, 128], P(('face', 'tile')), may hold values from -0.5 to 0.5
- block_dest: int32 [8192], P(('face', 'tile')), may hold values from 0 to 127, as said below
- block_row: int32 [8192], P(('face', 'tile')), may hold values from 0 to 15
- tracers: float32 [250, 4, 128, 2048], P(None, None, 'face', 'tile'), may hold values from 0.1 to 10
- rate_coef: float32 [250, 12], replicated, may hold values from -1.75 to 1.75
- photo_coef: float32 [250], replicated, may hold values from 0.1 to 3
Outputs:
- met_tile: float32 [12, 4, 128, 2048], P(None, None, 'face', 'tile')
- species_out: float32 [250, 4, 128, 2048], P(None, None, 'face', 'tile')
The draws below stay inside these ranges and needn't reach their ends.
Inputs may be any that keep to these rules, and one draw needn't show every extreme that they name: `block_dest`: each source owner (the 64 blocks of one device) names any one tile owner at most 2 times; in every draw some tile owner is named exactly 2 times by every source owner.
All inputs are finite; a program needn't handle non-finite values.
Results may differ from the reference program's by a relative error of at most 0.0029.
Values may be sent and summed in bfloat16 or wider, within the bound.
A program may use at most 128 MiB of HBM per device.

```python
import math
import jax
import jax.numpy as jnp
from jax import lax

NFLD = 12
NSPEC = 250
LEV = 4
TY = 128
TX = 16
CAP = 2
ADV_STEPS = 2
SB = 64
SRCBLK = 8192
FL = 48
NX = 128
NY = 2048
N_FACE = 8
N_TILE = 16


def draw_block_dest(key, part):
    owners = N_FACE * N_TILE
    hottest = jax.random.randint(jax.random.fold_in(key, 7), (), 0, owners)

    def one_source(source_key):
        others = jax.random.permutation(source_key, owners - 1)
        shuffle = jax.random.permutation(jax.random.fold_in(source_key, 3), SB)
        position = jnp.arange(SB)
        group_index = jnp.clip((position - CAP) // CAP, 0, owners - 2)
        chosen = jnp.where(position < CAP, hottest, (hottest + 1 + others[group_index]) % owners)
        return chosen[shuffle]
    source_keys = jax.random.split(jax.random.fold_in(key, 11), owners)
    return jax.vmap(one_source)(source_keys).reshape(owners * SB).astype(jnp.int32)


def set_ends(entries, rng, low, high):
    index_at = [jax.random.randint(jax.random.fold_in(rng, axis), (), 0, length) for axis, length in enumerate(entries.shape)]
    longest = entries.shape.index(max(entries.shape))
    beside = index_at[:longest] + [(index_at[longest] + 1) % entries.shape[longest]] + index_at[longest + 1:]
    return entries.at[tuple(index_at)].set(low).at[tuple(beside)].set(high)


def steps_of(key, extent, cuts, low, top_value):
    def one(dim, parts):
        steps = jax.random.uniform(jax.random.fold_in(jax.random.fold_in(key, 6), dim), (parts,), jnp.float32, low / len(cuts), top_value / len(cuts))
        return jnp.repeat(jnp.exp(steps), extent[dim] // parts).reshape((-1,) + (1,) * (len(extent) - dim - 1))

    factor_of = one(*cuts[0])
    for cut in cuts[1:]:
        factor_of = factor_of * one(*cut)
    return factor_of


def normal_values(rng, shape, width, limit, pieces=(), dtype=jnp.bfloat16):
    result = width * jax.random.normal(rng, shape, jnp.float32)
    if pieces:
        result = result * steps_of(rng, shape, pieces, -0.22, 0.18)
    return jnp.clip(result, -limit, limit).astype(dtype)


def setup_inputs(seed: int = 0) -> dict:
    splits = jax.random.split(jax.random.key(seed), 8)
    return {
        "met_src": normal_values(splits[0], (SRCBLK, FL, TY), 1.0, 6.0, ((0, 128),)),
        "intersection_weights": normal_values(splits[1], (SRCBLK, TY, TY), TY ** -0.5, 0.5, ((0, 128),)),
        "block_dest": draw_block_dest(jax.random.fold_in(splits[7], 71), 0),
        "block_row": set_ends(jax.random.randint(splits[3], (SRCBLK,), 0, TX), jax.random.fold_in(splits[3], 1), 0, TX - 1).astype(jnp.int32),
        "tracers": jnp.clip(jnp.exp(math.log(10.0) - 4.6051702 * jax.random.uniform(splits[4], (NSPEC, LEV, NX, NY), jnp.float32) ** steps_of(splits[4], (NSPEC, LEV, NX, NY), ((2, 8), (3, 16)), -0.2, 0.2)), 0.1, 10.0),
        "rate_coef": normal_values(splits[5], (NSPEC, NFLD), NFLD ** -0.5, 1.75, (), jnp.float32),
        "photo_coef": jnp.clip(jnp.exp(jax.random.uniform(splits[6], (NSPEC,), jnp.float32, math.log(0.1), math.log(3.0))), 0.1, 3.0),
    }


def reference(met_src, intersection_weights, block_dest, block_row, tracers, rate_coef, photo_coef):
    products = jnp.einsum("sfi,sij->sfj", met_src.astype(jnp.float32), intersection_weights.astype(jnp.float32), precision=lax.Precision.HIGHEST)
    products = lax.optimization_barrier(products.astype(jnp.bfloat16)).astype(jnp.float32)
    target_rows = (block_dest * TX + block_row).astype(jnp.int32)
    summed = jax.ops.segment_sum(products, target_rows, num_segments=N_FACE * N_TILE * TX)
    met_tile = summed.reshape(N_FACE, N_TILE, TX, NFLD, LEV, TY).transpose(3, 4, 0, 2, 1, 5).reshape(NFLD, LEV, NX, NY)
    courant_x = 0.3 * jnp.tanh(met_tile[0])
    courant_y = 0.3 * jnp.tanh(met_tile[1])
    column_depth = jnp.cumsum(jax.nn.softplus(met_tile[2]), axis=0)
    light = jnp.exp(-column_depth)

    def one_species(species_item):
        amount, coefficients, photolysis = species_item
        for substep in range(ADV_STEPS):
            flux_x = jnp.maximum(courant_x, 0.0) * amount + jnp.minimum(courant_x, 0.0) * jnp.roll(amount, -1, axis=1)
            flux_y = jnp.maximum(courant_y, 0.0) * amount + jnp.minimum(courant_y, 0.0) * jnp.roll(amount, -1, axis=2)
            amount = amount - (flux_x - jnp.roll(flux_x, 1, axis=1)) - (flux_y - jnp.roll(flux_y, 1, axis=2))
        exponent = jnp.einsum("f,flxy->lxy", coefficients, met_tile, precision=lax.Precision.HIGHEST) + photolysis * light
        return amount / (1.0 + jax.nn.softplus(exponent))

    species_out = lax.map(one_species, (tracers, rate_coef, photo_coef))
    return met_tile, species_out
```

```python
import functools
import jax
import jax.numpy as jnp
from jax import lax
from jax.experimental import pallas as pl
from jax.experimental.pallas import tpu as pltpu
from jax.sharding import PartitionSpec as P

MESH = pl.DeviceIdType.MESH
F32 = jnp.float32
BF16 = jnp.bfloat16
PARTS = (("x", "y", "z"), ("y", "z", "x"), ("z", "x", "y"))
RING = 4
ITEMS = 64
SLAB = 16 + 16 * ITEMS
CUT = 16 + 8 * ITEMS
PER_PART = 22


def whereabouts():
    face = lax.axis_index("face")
    tile = lax.axis_index("tile")
    return {"x": lax.rem(tile, 4), "y": face // 2, "z": tile // 4, "c": lax.rem(face, 2)}


def device(at):
    return (at["y"] * 2 + at["c"], at["z"] * 4 + at["x"])


def moved(at, dim, by):
    there = dict(at)
    there[dim] = 1 - at[dim] if dim == "c" else lax.rem(at[dim] + by, RING)
    return there


class Copies:
    def __init__(self, send, recv):
        self.send, self.recv, self.made = send, recv, {}

    def start(self, index, src, dst, there):
        copy = pltpu.make_async_remote_copy(
            src_ref=src,
            dst_ref=dst,
            send_sem=self.send.at[index],
            recv_sem=self.recv.at[index],
            device_id=device(there),
            device_id_type=MESH,
        )
        copy.start()
        self.made[index] = copy

    def arrived(self, *indices):
        for index in indices:
            self.made[index].wait_recv()

    def sent(self):
        for copy in self.made.values():
            copy.wait_send()


def regrid(at, copies, met_ref, weight_ref, key_ref, mx_ref, cs, gath, mask, part_sum, relay, ring_in, full, cut_sum, last_in):
    me = {p: at[dims[0]] * 2 + at["c"] for p, dims in enumerate(PARTS)}
    low, high = pl.ds(0, CUT), pl.ds(CUT, SLAB - CUT)

    for p, (first, second, third) in enumerate(PARTS):
        base, own = p * PER_PART, gath.at[p, me[p]]
        nxt, prv, mate = moved(at, first, 1), moved(at, first, 3), moved(at, "c", 1)
        gath[p, me[p], 0:16, :] = key_ref[p]
        gath[p, me[p], 16:SLAB, :] = cs[p * 1024 : (p + 1) * 1024, :].astype(BF16)
        copies.start(base + 0, own.at[low], own.at[low], nxt)
        copies.start(base + 2, own.at[high], own.at[high], prv)
        copies.start(base + 1, own.at[high], own.at[high], nxt)
        copies.start(base + 3, own.at[low], own.at[low], prv)
        copies.start(base + 4, own, own, mate)

    def pass_on(p, wait, half, step, index, there):
        base = p * PER_PART
        slot = lax.rem(at[PARTS[p][0]] + step, RING) * 2 + at["c"]
        ref = gath.at[p, slot, half]
        if wait is not None:
            copies.arrived(base + wait)
        copies.start(base + index, ref, ref, there)

    for p, (first, second, third) in enumerate(PARTS):
        pass_on(p, 0, low, 3, 5, moved(at, first, 1))
        pass_on(p, None, low, 3, 6, moved(at, "c", 1))
        pass_on(p, 2, high, 1, 7, moved(at, first, 3))
        pass_on(p, None, high, 1, 8, moved(at, "c", 1))
    for p, (first, second, third) in enumerate(PARTS):
        pass_on(p, 1, high, 3, 9, moved(at, "c", 1))
        pass_on(p, 3, low, 1, 10, moved(at, "c", 1))
    for p, (first, second, third) in enumerate(PARTS):
        pass_on(p, 5, low, 2, 11, moved(at, "c", 1))
        pass_on(p, 7, high, 2, 12, moved(at, "c", 1))

    lane = lax.broadcasted_iota(jnp.int32, (1, 128), 1)
    rows = lax.broadcasted_iota(jnp.int32, (256, 128), 0).astype(F32)
    h0, h1 = pl.ds(0, 512), pl.ds(512, 512)

    for p, (first, second, third) in enumerate(PARTS):
        base = p * PER_PART
        copies.arrived(*[base + k for k in (4, 6, 8, 9, 10, 11, 12)])
        mine = me[p].astype(F32)
        for a in range(RING):
            k0 = gath[p, 2 * a, 0:16, :].astype(F32)
            k1 = gath[p, 2 * a + 1, 0:16, :].astype(F32)
            high_key = jnp.where(lane < ITEMS, k0[0:1, :], k1[0:1, :])
            low_key = jnp.where(lane < ITEMS, k0[8:9, :], k1[8:9, :])
            key = jnp.where(high_key == mine, low_key, -1.0)
            mask[:, a * 128 : (a + 1) * 128] = jnp.where(rows == key, 1.0, 0.0).astype(BF16)

        @pl.loop(0, 8)
        def _(pair):
            def level(fl):
                start = pl.multiple_of(16 + fl * ITEMS, 16)
                return jnp.concatenate([gath[p, s, pl.ds(start, ITEMS), :] for s in range(8)], axis=0)

            rhs = jnp.concatenate([level(2 * pair), level(2 * pair + 1)], axis=1)
            out = jnp.dot(mask[...], rhs, preferred_element_type=F32).astype(BF16)
            for side in range(2):
                start = pl.multiple_of((2 * pair + side) * 64, 64)
                for b in range(RING):
                    part_sum[p, b, pl.ds(start, 64), :] = out[b * 64 : (b + 1) * 64, side * 128 : (side + 1) * 128]

        nxt, prv = moved(at, second, 1), moved(at, second, 3)
        up, down, far = nxt[second], prv[second], lax.rem(at[second] + 2, RING)
        copies.start(base + 13, part_sum.at[p, far, h0], relay.at[p, 0], nxt)
        copies.start(base + 14, part_sum.at[p, far, h1], relay.at[p, 1], prv)
        copies.start(base + 15, part_sum.at[p, up, h1], ring_in.at[p, 0, h1], nxt)
        copies.start(base + 16, part_sum.at[p, down, h0], ring_in.at[p, 1, h0], prv)

    for p, (first, second, third) in enumerate(PARTS):
        base = p * PER_PART
        nxt, prv = moved(at, second, 1), moved(at, second, 3)
        for index, side, there, half in ((13, 0, nxt, h0), (14, 1, prv, h1)):
            copies.arrived(base + index)
            to = there[second]
            total = part_sum[p, to, half, :].astype(F32) + relay[p, side].astype(F32)
            part_sum[p, to, half, :] = total.astype(BF16)
            copies.start(base + index + 4, part_sum.at[p, to, half], ring_in.at[p, side, half], there)

    for p, (first, second, third) in enumerate(PARTS):
        base = p * PER_PART
        copies.arrived(*[base + k for k in (15, 16, 17, 18)])
        own = at[second]

        @pl.loop(0, 16)
        def _(fl):
            start = pl.multiple_of(fl * 64, 64)
            block = pl.ds(start, 64)
            total = part_sum[p, own, block, :].astype(F32) + ring_in[p, 0, block, :].astype(F32) + ring_in[p, 1, block, :].astype(F32)
            full[p, block, :] = total
            narrow = total.astype(BF16)
            for c in range(RING):
                cut_sum[p, c, pl.ds(pl.multiple_of(fl * 16, 16), 16), :] = narrow[c * 16 : (c + 1) * 16, :]

        for k, by in enumerate((1, 3, 2)):
            there = moved(at, third, by)
            copies.start(base + 19 + k, cut_sum.at[p, there[third]], last_in.at[p, k], there)

    for p, (first, second, third) in enumerate(PARTS):
        base = p * PER_PART
        copies.arrived(base + 19, base + 20, base + 21)
        for fl in range(16):
            start = pl.multiple_of(fl * 64 + at[third] * 16, 16)
            here = slice(fl * 16, fl * 16 + 16)
            total = full[p, pl.ds(start, 16), :]
            for k in range(3):
                total = total + last_in[p, k, here, :].astype(F32)
            mx_ref[p * 256 + fl * 16 : p * 256 + fl * 16 + 16, :] = total


def contributions(met_ref, weight_ref, cs):
    @pl.loop(0, ITEMS // 4)
    def _(group):
        for k in range(4):
            s = group * 4 + k
            cs[pl.ds(s, 48, stride=ITEMS), :] = jnp.dot(met_ref[s], weight_ref[s], preferred_element_type=F32)


def greet(at):
    barrier = pltpu.get_barrier_semaphore()
    peers = [moved(at, dim, by) for dim in ("x", "y", "z") for by in (1, 2, 3)] + [moved(at, "c", 1)]
    for there in peers:
        pl.semaphore_signal(barrier, inc=1, device_id=device(there), device_id_type=MESH)
    return barrier, len(peers)


REGRID_SCRATCH = [
    pltpu.VMEM((48 * ITEMS, 128), F32),
    pltpu.VMEM((3, 8, SLAB, 128), BF16),
    pltpu.VMEM((256, 512), BF16),
    pltpu.VMEM((3, RING, 1024, 128), BF16),
    pltpu.VMEM((3, 2, 512, 128), BF16),
    pltpu.VMEM((3, 2, 1024, 128), BF16),
    pltpu.VMEM((3, 1024, 128), F32),
    pltpu.VMEM((3, RING, 256, 128), BF16),
    pltpu.VMEM((3, 3, 256, 128), BF16),
]


def keys_of(block_dest, block_row):
    face, tile = block_dest >> 4, block_dest & 15
    pos = {"x": tile & 3, "y": face >> 1, "z": tile >> 2}
    out = []
    for first, second, third in PARTS:
        high = pos[first] * 2 + (face & 1)
        low = pos[second] * 64 + pos[third] * 16 + block_row
        both = jnp.stack([high, low])[:, None, :]
        both = jnp.broadcast_to(both, (2, 8, ITEMS)).reshape(16, ITEMS)
        out.append(jnp.concatenate([both, both], axis=1))
    return jnp.stack(out).astype(BF16)


def regrid_kernel(met_ref, weight_ref, key_ref, mx_ref, send, recv, *scratch):
    at = whereabouts()
    barrier, count = greet(at)
    contributions(met_ref, weight_ref, scratch[0])
    pl.semaphore_wait(barrier, count)
    copies = Copies(send, recv)
    regrid(at, copies, met_ref, weight_ref, key_ref, mx_ref, *scratch)
    copies.sent()
    mx_ref[768:1024, :] = jnp.zeros((256, 128), F32)


def regrid_call(met_src, weights, keys):
    vmem = pl.BlockSpec(memory_space=pltpu.VMEM)
    return pl.pallas_call(
        regrid_kernel,
        out_shape=jax.ShapeDtypeStruct((1024, 128), F32),
        in_specs=[vmem] * 3,
        out_specs=vmem,
        scratch_shapes=[pltpu.SemaphoreType.DMA((66,)), pltpu.SemaphoreType.DMA((66,))] + REGRID_SCRATCH,
        compiler_params=pltpu.CompilerParams(collective_id=0, has_side_effects=True, vmem_limit_bytes=50 << 20),
        name="regrid",
    )(met_src, weights, keys)


ADV_STEPS = 2


def from_behind(shard, axis, by):
    devices = lax.axis_size(axis)
    return lax.ppermute(shard, axis, [(i, (i + by) % devices) for i in range(devices)])


def with_halo(block, sides, width):
    for axis, dim in sides:
        count = lax.axis_size(axis)
        forward = [(i, i + 1) for i in range(count - 1)]
        forward.append((count - 1, 0))
        backward = [(target, source) for source, target in forward]
        low = lax.ppermute(
            lax.slice_in_dim(block, block.shape[dim] - width, None, axis=dim), axis, forward
        )
        high = lax.ppermute(lax.slice_in_dim(block, 0, width, axis=dim), axis, backward)
        block = jnp.concatenate([low, block, high], axis=dim)
    return block


def local(met_src, intersection_weights, block_dest, block_row, tracers, rate_coef, photo_coef):
    levfields = met_src.shape[1]
    nfields = rate_coef.shape[1]
    levels = levfields // nfields
    rows_x, cell_count = tracers.shape[2], tracers.shape[3]
    mx = regrid_call(met_src, intersection_weights, keys_of(block_dest, block_row))
    met_tile = mx[:768].reshape(nfields, levels, rows_x, cell_count)
    courant_x = 0.3 * jnp.tanh(met_tile[0])
    courant_y = 0.3 * jnp.tanh(met_tile[1])
    west_row = from_behind(courant_x[:, -1:, :], "face", 1)
    south_column = from_behind(courant_y[:, :, -1:], "tile", 1)
    courant_xe = jnp.concatenate([west_row, courant_x], axis=1)
    courant_ye = jnp.concatenate([south_column, courant_y], axis=2)
    amount = tracers
    for substep in range(ADV_STEPS):
        padded = with_halo(amount, (("face", 2), ("tile", 3)), 1)
        lower_x = padded[:, :, 0 : rows_x + 1, 1:-1]
        upper_x = padded[:, :, 1 : rows_x + 2, 1:-1]
        flux_x = jnp.maximum(courant_xe, 0.0) * lower_x + jnp.minimum(courant_xe, 0.0) * upper_x
        lower_y = padded[:, :, 1:-1, 0 : cell_count + 1]
        upper_y = padded[:, :, 1:-1, 1 : cell_count + 2]
        flux_y = jnp.maximum(courant_ye, 0.0) * lower_y + jnp.minimum(courant_ye, 0.0) * upper_y
        amount = (
            padded[:, :, 1:-1, 1:-1]
            - (flux_x[:, :, 1:, :] - flux_x[:, :, :-1, :])
            - (flux_y[:, :, :, 1:] - flux_y[:, :, :, :-1])
        )
    column_depth = jnp.cumsum(jax.nn.softplus(met_tile[2]), axis=0)
    light = jnp.exp(-column_depth)
    exponent = (
        jnp.einsum("sf,flxy->slxy", rate_coef, met_tile, precision=lax.Precision.HIGHEST)
        + photo_coef[:, None, None, None] * light[None]
    )
    species_out = amount / (1.0 + jax.nn.softplus(exponent))
    return (met_tile, species_out)


def solution(mesh):
    return jax.shard_map(
        local,
        mesh=mesh,
        in_specs=(
            P(("face", "tile"), None, None),
            P(("face", "tile"), None, None),
            P(("face", "tile")),
            P(("face", "tile")),
            P(None, None, "face", "tile"),
            P(),
            P(),
        ),
        out_specs=(P(None, None, "face", "tile"), P(None, None, "face", "tile")),
        check_vma=False,
    )
```

```python
import functools
import jax
import jax.numpy as jnp
from jax import lax
from jax.experimental import pallas as pl
from jax.experimental.pallas import tpu as pltpu
from jax.sharding import PartitionSpec as P

MESH = pl.DeviceIdType.MESH
F32 = jnp.float32
BF16 = jnp.bfloat16
PARTS = (("x", "y", "z"), ("y", "z", "x"), ("z", "x", "y"))
RING = 4
ITEMS = 64
SLAB = 16 + 16 * ITEMS
CUT = 16 + 8 * ITEMS
PER_PART = 22


def whereabouts():
    face = lax.axis_index("face")
    tile = lax.axis_index("tile")
    return {"x": lax.rem(tile, 4), "y": face // 2, "z": tile // 4, "c": lax.rem(face, 2)}


def device(at):
    return (at["y"] * 2 + at["c"], at["z"] * 4 + at["x"])


def moved(at, dim, by):
    there = dict(at)
    there[dim] = 1 - at[dim] if dim == "c" else lax.rem(at[dim] + by, RING)
    return there


class Copies:
    def __init__(self, send, recv):
        self.send, self.recv, self.made, self.over = send, recv, {}, set()

    def start(self, index, src, dst, there):
        copy = pltpu.make_async_remote_copy(
            src_ref=src,
            dst_ref=dst,
            send_sem=self.send.at[index],
            recv_sem=self.recv.at[index],
            device_id=device(there) if isinstance(there, dict) else there,
            device_id_type=MESH,
        )
        copy.start()
        self.made[index] = copy

    def arrived(self, *indices):
        for index in indices:
            self.made[index].wait_recv()

    def sent_of(self, *indices):
        for index in indices:
            self.made[index].wait_send()
            self.over.add(index)

    def sent(self):
        self.sent_of(*[index for index in self.made if index not in self.over])


def regrid(at, copies, met_ref, weight_ref, key_ref, mx_ref, cs, gath, mask, part_sum, relay, ring_in, full, cut_sum, last_in, meanwhile):
    me = {p: at[dims[0]] * 2 + at["c"] for p, dims in enumerate(PARTS)}
    low, high = pl.ds(0, CUT), pl.ds(CUT, SLAB - CUT)

    for p, (first, second, third) in enumerate(PARTS):
        base, own = p * PER_PART, gath.at[p, me[p]]
        nxt, prv, mate = moved(at, first, 1), moved(at, first, 3), moved(at, "c", 1)
        gath[p, me[p], 0:16, :] = key_ref[p]
        gath[p, me[p], 16:SLAB, :] = cs[p * 1024 : (p + 1) * 1024, :].astype(BF16)
        copies.start(base + 0, own.at[low], own.at[low], nxt)
        copies.start(base + 2, own.at[high], own.at[high], prv)
        copies.start(base + 1, own.at[high], own.at[high], nxt)
        copies.start(base + 3, own.at[low], own.at[low], prv)
        copies.start(base + 4, own, own, mate)

    def pass_on(p, wait, half, step, index, there):
        base = p * PER_PART
        slot = lax.rem(at[PARTS[p][0]] + step, RING) * 2 + at["c"]
        ref = gath.at[p, slot, half]
        if wait is not None:
            copies.arrived(base + wait)
        copies.start(base + index, ref, ref, there)

    for p, (first, second, third) in enumerate(PARTS):
        pass_on(p, 0, low, 3, 5, moved(at, first, 1))
        pass_on(p, None, low, 3, 6, moved(at, "c", 1))
        pass_on(p, 2, high, 1, 7, moved(at, first, 3))
        pass_on(p, None, high, 1, 8, moved(at, "c", 1))
    meanwhile()
    for p, (first, second, third) in enumerate(PARTS):
        pass_on(p, 1, high, 3, 9, moved(at, "c", 1))
        pass_on(p, 3, low, 1, 10, moved(at, "c", 1))
    for p, (first, second, third) in enumerate(PARTS):
        pass_on(p, 5, low, 2, 11, moved(at, "c", 1))
        pass_on(p, 7, high, 2, 12, moved(at, "c", 1))

    lane = lax.broadcasted_iota(jnp.int32, (1, 128), 1)
    rows = lax.broadcasted_iota(jnp.int32, (256, 128), 0).astype(F32)
    h0, h1 = pl.ds(0, 512), pl.ds(512, 512)

    for p, (first, second, third) in enumerate(PARTS):
        base = p * PER_PART
        copies.arrived(*[base + k for k in (4, 6, 8, 9, 10, 11, 12)])
        mine = me[p].astype(F32)
        for a in range(RING):
            k0 = gath[p, 2 * a, 0:16, :].astype(F32)
            k1 = gath[p, 2 * a + 1, 0:16, :].astype(F32)
            high_key = jnp.where(lane < ITEMS, k0[0:1, :], k1[0:1, :])
            low_key = jnp.where(lane < ITEMS, k0[8:9, :], k1[8:9, :])
            key = jnp.where(high_key == mine, low_key, -1.0)
            mask[:, a * 128 : (a + 1) * 128] = jnp.where(rows == key, 1.0, 0.0).astype(BF16)

        @pl.loop(0, 8)
        def _(pair):
            def level(fl):
                start = pl.multiple_of(16 + fl * ITEMS, 16)
                return jnp.concatenate([gath[p, s, pl.ds(start, ITEMS), :] for s in range(8)], axis=0)

            rhs = jnp.concatenate([level(2 * pair), level(2 * pair + 1)], axis=1)
            out = jnp.dot(mask[...], rhs, preferred_element_type=F32).astype(BF16)
            for side in range(2):
                start = pl.multiple_of((2 * pair + side) * 64, 64)
                for b in range(RING):
                    part_sum[p, b, pl.ds(start, 64), :] = out[b * 64 : (b + 1) * 64, side * 128 : (side + 1) * 128]

        nxt, prv = moved(at, second, 1), moved(at, second, 3)
        up, down, far = nxt[second], prv[second], lax.rem(at[second] + 2, RING)
        copies.start(base + 13, part_sum.at[p, far, h0], relay.at[p, 0], nxt)
        copies.start(base + 14, part_sum.at[p, far, h1], relay.at[p, 1], prv)
        copies.start(base + 15, part_sum.at[p, up, h1], ring_in.at[p, 0, h1], nxt)
        copies.start(base + 16, part_sum.at[p, down, h0], ring_in.at[p, 1, h0], prv)

    for p, (first, second, third) in enumerate(PARTS):
        base = p * PER_PART
        nxt, prv = moved(at, second, 1), moved(at, second, 3)
        for index, side, there, half in ((13, 0, nxt, h0), (14, 1, prv, h1)):
            copies.arrived(base + index)
            to = there[second]
            total = part_sum[p, to, half, :].astype(F32) + relay[p, side].astype(F32)
            part_sum[p, to, half, :] = total.astype(BF16)
            copies.start(base + index + 4, part_sum.at[p, to, half], ring_in.at[p, side, half], there)

    for p, (first, second, third) in enumerate(PARTS):
        base = p * PER_PART
        copies.arrived(*[base + k for k in (15, 16, 17, 18)])
        own = at[second]

        @pl.loop(0, 16)
        def _(fl):
            start = pl.multiple_of(fl * 64, 64)
            block = pl.ds(start, 64)
            total = part_sum[p, own, block, :].astype(F32) + ring_in[p, 0, block, :].astype(F32) + ring_in[p, 1, block, :].astype(F32)
            full[p, block, :] = total
            narrow = total.astype(BF16)
            for c in range(RING):
                cut_sum[p, c, pl.ds(pl.multiple_of(fl * 16, 16), 16), :] = narrow[c * 16 : (c + 1) * 16, :]

        for k, by in enumerate((1, 3, 2)):
            there = moved(at, third, by)
            copies.start(base + 19 + k, cut_sum.at[p, there[third]], last_in.at[p, k], there)

    for p, (first, second, third) in enumerate(PARTS):
        base = p * PER_PART
        copies.arrived(base + 19, base + 20, base + 21)
        for fl in range(16):
            start = pl.multiple_of(fl * 64 + at[third] * 16, 16)
            here = slice(fl * 16, fl * 16 + 16)
            total = full[p, pl.ds(start, 16), :]
            for k in range(3):
                total = total + last_in[p, k, here, :].astype(F32)
            mx_ref[p * 256 + fl * 16 : p * 256 + fl * 16 + 16, :] = total


def contributions(met_ref, weight_ref, cs):
    @pl.loop(0, ITEMS // 4)
    def _(group):
        for k in range(4):
            s = group * 4 + k
            cs[pl.ds(s, 48, stride=ITEMS), :] = jnp.dot(met_ref[s], weight_ref[s], preferred_element_type=F32)


def greet(at, near):
    barrier = pltpu.get_barrier_semaphore()
    peers = [moved(at, dim, by) for dim in ("x", "y", "z") for by in (1, 2, 3)] + [moved(at, "c", 1)]
    peers = [device(there) for there in peers] + [near[side] for side in "nsew"]
    for there in peers:
        pl.semaphore_signal(barrier, inc=1, device_id=there, device_id_type=MESH)
    return barrier, len(peers)


REGRID_SCRATCH = [
    pltpu.VMEM((48 * ITEMS, 128), F32),
    pltpu.VMEM((3, 8, SLAB, 128), BF16),
    pltpu.VMEM((256, 512), BF16),
    pltpu.VMEM((3, RING, 1024, 128), BF16),
    pltpu.VMEM((3, 2, 512, 128), BF16),
    pltpu.VMEM((3, 2, 1024, 128), BF16),
    pltpu.VMEM((3, 1024, 128), F32),
    pltpu.VMEM((3, RING, 256, 128), BF16),
    pltpu.VMEM((3, 3, 256, 128), BF16),
]


def keys_of(block_dest, block_row):
    face, tile = block_dest >> 4, block_dest & 15
    pos = {"x": tile & 3, "y": face >> 1, "z": tile >> 2}
    out = []
    for first, second, third in PARTS:
        high = pos[first] * 2 + (face & 1)
        low = pos[second] * 64 + pos[third] * 16 + block_row
        both = jnp.stack([high, low])[:, None, :]
        both = jnp.broadcast_to(both, (2, 8, ITEMS)).reshape(16, ITEMS)
        out.append(jnp.concatenate([both, both], axis=1))
    return jnp.stack(out).astype(BF16)


SPECIES = 256
HALO_COPIES = 66


def lanes_of(shape, dim):
    return lax.broadcasted_iota(jnp.int32, shape, dim)


def edge_picker(pick):
    row, lane = lanes_of((128, 128), 0), lanes_of((128, 128), 1)
    for r in range(16):
        east = jnp.logical_and(row == 127, lane == 2 * r)
        west = jnp.logical_and(row == 0, lane == 2 * r + 1)
        pick[r * 128 : (r + 1) * 128, :] = jnp.where(jnp.logical_or(east, west), 1.0, 0.0).astype(BF16)


def picked_edges(narrow, pick, l):
    rows = jnp.concatenate([narrow[l, r] for r in range(16)], axis=1)
    return jnp.dot(rows, pick[...], preferred_element_type=F32).astype(BF16)


def neighbours():
    face, tile = lax.axis_index("face"), lax.axis_index("tile")
    return {
        "n": (lax.rem(face + 1, 8), tile),
        "s": (lax.rem(face + 7, 8), tile),
        "e": (face, lax.rem(tile + 1, 16)),
        "w": (face, lax.rem(tile + 15, 16)),
    }


def start_tracers(tracer_ref, amount, load):
    count = tracer_ref.shape[0]
    copies = []
    for lr in range(64):
        copy = pltpu.make_async_copy(
            tracer_ref.at[:, lr, 0], amount.at[lr // 16, lr % 16 + 1, pl.ds(0, count)], load.at[lr]
        )
        copy.start()
        copies.append(copy)
    return copies


def first_halos(near, copies, loads, amount, narrow, pick, edges, row_in, edge_in):
    for copy in loads:
        copy.wait()
    count = 250

    @pl.loop(0, 64)
    def _(lr):
        narrow[lr // 16, lax.rem(lr, 16)] = amount[lr // 16, lax.rem(lr, 16) + 1].astype(BF16)

    copies.start(HALO_COPIES + 0, narrow.at[:, 15], row_in.at[0, 0], near["n"])
    copies.start(HALO_COPIES + 1, narrow.at[:, 0], row_in.at[0, 1], near["s"])

    @pl.loop(0, 4)
    def _(l):
        edges[0, l] = picked_edges(narrow, pick, l)

    copies.start(HALO_COPIES + 2, edges.at[0], edge_in.at[0, 0], near["e"])
    copies.start(HALO_COPIES + 3, edges.at[0], edge_in.at[0, 1], near["w"])


def coefficients(near, copies, mx_ref, courant, courant_in, shifted, coef, band):
    courant[0] = 0.3 * jnp.tanh(mx_ref[0:64, :])
    courant[1] = 0.3 * jnp.tanh(mx_ref[64:128, :])
    copies.start(HALO_COPIES + 4, courant.at[0], courant_in.at[0], near["n"])
    copies.start(HALO_COPIES + 5, courant.at[1], courant_in.at[1], near["e"])

    depth = jnp.zeros((16, 128), F32)
    for l in range(4):
        value = mx_ref[128 + l * 16 : 144 + l * 16, :]
        depth = depth + (jnp.maximum(value, 0.0) + jnp.log1p(jnp.exp(-jnp.abs(value))))
        mx_ref[768 + l * 16 : 784 + l * 16, :] = jnp.exp(-depth)
    mx_ref[832:1024, :] = jnp.zeros((192, 128), F32)

    row, lane = lanes_of((128, 128), 0), lanes_of((128, 128), 1)
    from_west = jnp.where(row == lane - 1, 1.0, 0.0)
    from_east = jnp.where(row == lane + 1, 1.0, 0.0)
    sub, edge = lanes_of((16, 128), 0), lanes_of((16, 128), 1)
    copies.arrived(HALO_COPIES + 4, HALO_COPIES + 5)
    for l in range(4):
        rows = slice(l * 16, l * 16 + 16)
        shifted[l, 8:24, :] = courant[0, rows, :]
        shifted[l, 7:8, :] = courant_in[0, l * 16 + 15 : l * 16 + 16, :]
        cx, cy = courant[0, rows, :], courant[1, rows, :]
        behind_x = shifted[l, 7:23, :]
        behind_y = jnp.where(edge == 0, pltpu.roll(courant_in[1, rows, :], 1, 1), pltpu.roll(cy, 1, 1))
        coef[l, 0] = 1.0 - jnp.maximum(cx, 0.0) + jnp.minimum(behind_x, 0.0) - jnp.maximum(cy, 0.0) + jnp.minimum(behind_y, 0.0)
        coef[l, 1] = jnp.maximum(behind_x, 0.0)
        coef[l, 2] = -jnp.minimum(cx, 0.0)
        west, east = jnp.maximum(behind_y, 0.0), -jnp.minimum(cy, 0.0)
        for r in range(16):
            w, e = west[r : r + 1, :], east[r : r + 1, :]
            band[l, r, 0:128, :] = (from_west * w + from_east * e).astype(BF16)
            k = 2 * r % 16
            ends = jnp.where(jnp.logical_and(sub == k, edge == 0), w, jnp.where(jnp.logical_and(sub == k + 1, edge == 127), e, 0.0))
            other = 128 + 16 * (1 - r // 8)
            band[l, r, 128 + 16 * (r // 8) : 144 + 16 * (r // 8), :] = ends.astype(BF16)
            band[l, r, other : other + 16, :] = jnp.zeros((16, 128), BF16)


def advance(source, target, narrow, side, coef, band, row_in, edge_in, step, l, keep):
    source[l, 0] = row_in[step, 0, l].astype(F32)
    source[l, 17] = row_in[step, 1, l].astype(F32)
    even = lax.rem(lanes_of((SPECIES, 128), 1), 2) == 0
    side[...] = jnp.where(even, edge_in[step, 0, l].astype(F32), edge_in[step, 1, l].astype(F32)).astype(BF16)

    @pl.loop(0, 16)
    def _(r):
        lhs = jnp.concatenate([narrow[l, r], side[...]], axis=1)
        across = jnp.dot(lhs, band[l, r], preferred_element_type=F32)
        total = coef[l, 0, pl.ds(r, 1), :] * source[l, r + 1] + coef[l, 1, pl.ds(r, 1), :] * source[l, r]
        total = total + coef[l, 2, pl.ds(r, 1), :] * source[l, r + 2] + across
        target[l, r + 1] = total
        if keep:
            narrow[l, r] = total.astype(BF16)


def advect(near, copies, adv_ref, amount, middle, narrow, side, pick, edges, coef, band, row_in, edge_in, store):
    copies.arrived(*[HALO_COPIES + k for k in range(4)])
    copies.sent_of(HALO_COPIES + 0, HALO_COPIES + 1)
    for l in range(4):
        advance(amount, middle, narrow, side, coef, band, row_in, edge_in, 0, l, True)
        base = HALO_COPIES + 6 + 4 * l
        copies.start(base + 0, narrow.at[l, 15], row_in.at[1, 0, l], near["n"])
        copies.start(base + 1, narrow.at[l, 0], row_in.at[1, 1, l], near["s"])
        edges[1, l] = picked_edges(narrow, pick, l)
        copies.start(base + 2, edges.at[1, l], edge_in.at[1, 0, l], near["e"])
        copies.start(base + 3, edges.at[1, l], edge_in.at[1, 1, l], near["w"])
    stores = []
    for l in range(4):
        base = HALO_COPIES + 6 + 4 * l
        copies.arrived(*[base + k for k in range(4)])
        advance(middle, amount, narrow, side, coef, band, row_in, edge_in, 1, l, False)
        copy = pltpu.make_async_copy(amount.at[l, pl.ds(1, 16)], adv_ref.at[l], store.at[l])
        copy.start()
        stores.append(copy)
    for copy in stores:
        copy.wait()


ADVECT_SCRATCH = [
    pltpu.VMEM((4, 18, SPECIES, 128), F32),
    pltpu.VMEM((4, 18, SPECIES, 128), F32),
    pltpu.VMEM((4, 16, SPECIES, 128), BF16),
    pltpu.VMEM((SPECIES, 128), BF16),
    pltpu.VMEM((2048, 128), BF16),
    pltpu.VMEM((2, 4, SPECIES, 128), BF16),
    pltpu.VMEM((2, 2, 4, SPECIES, 128), BF16),
    pltpu.VMEM((2, 2, 4, SPECIES, 128), BF16),
    pltpu.VMEM((2, 64, 128), F32),
    pltpu.VMEM((2, 64, 128), F32),
    pltpu.VMEM((4, 24, 128), F32),
    pltpu.VMEM((4, 3, 16, 128), F32),
    pltpu.VMEM((4, 16, 256, 128), BF16),
]
COPIES = HALO_COPIES + 22


def transport_kernel(met_ref, weight_ref, key_ref, tracer_ref, mx_ref, adv_ref, send, recv, load, store, *scratch):
    cut = len(REGRID_SCRATCH)
    regrid_scratch = scratch[:cut]
    amount, middle, narrow, side, pick, edges, row_in, edge_in, courant, courant_in, shifted, coef, band = scratch[cut:]
    at, near = whereabouts(), neighbours()
    loads = start_tracers(tracer_ref, amount, load)
    barrier, count = greet(at, near)
    contributions(met_ref, weight_ref, regrid_scratch[0])
    pl.semaphore_wait(barrier, count)
    copies = Copies(send, recv)

    def meanwhile():
        edge_picker(pick)

        @pl.loop(0, 64)
        def _(k):
            band[k // 16, lax.rem(k, 16), 128:256, :] = jnp.zeros((128, 128), BF16)

        first_halos(near, copies, loads, amount, narrow, pick, edges, row_in, edge_in)

    regrid(at, copies, met_ref, weight_ref, key_ref, mx_ref, *regrid_scratch, meanwhile=meanwhile)
    coefficients(near, copies, mx_ref, courant, courant_in, shifted, coef, band)
    advect(near, copies, adv_ref, amount, middle, narrow, side, pick, edges, coef, band, row_in, edge_in, store)
    copies.sent()


def transport_call(met_src, weights, keys, tracers):
    vmem, anywhere = pl.BlockSpec(memory_space=pltpu.VMEM), pl.BlockSpec(memory_space=pl.ANY)
    dma = pltpu.SemaphoreType.DMA
    return pl.pallas_call(
        transport_kernel,
        out_shape=(jax.ShapeDtypeStruct((1024, 128), F32), jax.ShapeDtypeStruct((4, 16, SPECIES, 128), F32)),
        in_specs=[vmem] * 3 + [anywhere],
        out_specs=(vmem, anywhere),
        scratch_shapes=[dma((COPIES,)), dma((COPIES,)), dma((64,)), dma((4,))] + REGRID_SCRATCH + ADVECT_SCRATCH,
        compiler_params=pltpu.CompilerParams(collective_id=0, has_side_effects=True, vmem_limit_bytes=60 << 20),
        name="transport",
    )(met_src, weights, keys, tracers)


CHUNK = 4


def chemistry_kernel(mx_ref, rate_ref, adv_ref, met_ref, out_ref, amount, result, load, store):
    chunks = 64 // CHUNK
    count = out_ref.shape[0]

    def fetch(k):
        rows = pl.ds(k * CHUNK, CHUNK)
        return pltpu.make_async_copy(adv_ref.at[rows], amount.at[rows], load.at[k])

    def put(lr):
        return pltpu.make_async_copy(result.at[lr, pl.ds(0, count)], out_ref.at[:, lr, 0], store.at[lr])

    for k in range(chunks):
        fetch(k).start()
    met_ref[...] = mx_ref[0:768, :]

    def fields(lr):
        value = mx_ref[pl.ds(lr, 16, stride=64), :]
        m1 = value.astype(BF16)
        rest = value - m1.astype(F32)
        m2 = rest.astype(BF16)
        m3 = (rest - m2.astype(F32)).astype(BF16)
        return jnp.concatenate([m1, m2, m3, m1, m2, m1], axis=0)

    @pl.loop(0, chunks)
    def _(k):
        fetch(k).wait()
        for pair in range(CHUNK // 2):
            lr = k * CHUNK + 2 * pair
            rhs = jnp.concatenate([fields(lr), fields(lr + 1)], axis=1)
            exponent = jnp.dot(rate_ref[...], rhs, preferred_element_type=F32)
            loss = jnp.maximum(exponent, 0.0) + jnp.log1p(jnp.exp(-jnp.abs(exponent)))
            for side in range(2):
                result[lr + side] = amount[lr + side] / (1.0 + loss[:, side * 128 : side * 128 + 128])
                put(lr + side).start()

    @pl.loop(0, 64)
    def _(lr):
        put(lr).wait()


def chemistry_call(mx, rates, adv, count):
    vmem, anywhere = pl.BlockSpec(memory_space=pltpu.VMEM), pl.BlockSpec(memory_space=pl.ANY)
    dma = pltpu.SemaphoreType.DMA
    return pl.pallas_call(
        chemistry_kernel,
        out_shape=(jax.ShapeDtypeStruct((768, 128), F32), jax.ShapeDtypeStruct((count, 64, 1, 128), F32)),
        in_specs=[vmem, vmem, anywhere],
        out_specs=(vmem, anywhere),
        scratch_shapes=[pltpu.VMEM((64, SPECIES, 128), F32), pltpu.VMEM((64, SPECIES, 128), F32), dma((64 // CHUNK,)), dma((64,))],
        compiler_params=pltpu.CompilerParams(vmem_limit_bytes=40 << 20),
        name="chemistry",
    )(mx, rates, adv)


def rates_of(rate_coef, photo_coef):
    both = jnp.concatenate([rate_coef, photo_coef[:, None]], axis=1)
    both = jnp.pad(both, ((0, SPECIES - both.shape[0]), (0, 16 - both.shape[1])))
    r1 = lax.reduce_precision(both, 8, 7)
    r2 = lax.reduce_precision(both - r1, 8, 7)
    r3 = both - r1 - r2
    return jnp.concatenate([r1, r1, r1, r2, r2, r3], axis=1).astype(BF16)


def local(met_src, intersection_weights, block_dest, block_row, tracers, rate_coef, photo_coef):
    species, levels, rows, cells = tracers.shape
    keys = keys_of(block_dest, block_row)
    rates = rates_of(rate_coef, photo_coef)
    mx, adv = transport_call(met_src, intersection_weights, keys, tracers.reshape(species, levels * rows, 1, cells))
    met, out = chemistry_call(mx, rates, adv.reshape(levels * rows, SPECIES, cells), species)
    return met.reshape(-1, levels, rows, cells), out.reshape(species, levels, rows, cells)


def solution(mesh):
    split = P(("face", "tile"))
    grid = P(None, None, "face", "tile")
    return jax.shard_map(
        local,
        mesh=mesh,
        in_specs=(split, split, split, split, grid, P(), P()),
        out_specs=(grid, grid),
        check_vma=False,
    )
```

```python
import functools
import jax
import jax.numpy as jnp
from jax import lax
from jax.experimental import pallas as pl
from jax.experimental.pallas import tpu as pltpu
from jax.sharding import PartitionSpec as P

MESH = pl.DeviceIdType.MESH
F32 = jnp.float32
BF16 = jnp.bfloat16
PARTS = (("x", "y", "z"), ("y", "z", "x"), ("z", "x", "y"))
RING = 4
ITEMS = 64
SLAB = 16 + 16 * ITEMS
CUT = 16 + 8 * ITEMS
PER_PART = 25


def whereabouts():
    face = lax.axis_index("face")
    tile = lax.axis_index("tile")
    return {"x": lax.rem(tile, 4), "y": face // 2, "z": tile // 4, "c": lax.rem(face, 2)}


def device(at):
    return (at["y"] * 2 + at["c"], at["z"] * 4 + at["x"])


def moved(at, dim, by):
    there = dict(at)
    there[dim] = 1 - at[dim] if dim == "c" else lax.rem(at[dim] + by, RING)
    return there


class Copies:
    def __init__(self, send, recv):
        self.send, self.recv, self.made, self.over = send, recv, {}, set()

    def start(self, index, src, dst, there):
        copy = pltpu.make_async_remote_copy(
            src_ref=src,
            dst_ref=dst,
            send_sem=self.send.at[index],
            recv_sem=self.recv.at[index],
            device_id=device(there) if isinstance(there, dict) else there,
            device_id_type=MESH,
        )
        copy.start()
        self.made[index] = copy

    def arrived(self, *indices):
        for index in indices:
            self.made[index].wait_recv()

    def sent_of(self, *indices):
        for index in indices:
            self.made[index].wait_send()
            self.over.add(index)

    def sent(self):
        self.sent_of(*[index for index in self.made if index not in self.over])


class Regrid:
    def __init__(self, at, copies, key_ref, mx_ref, cs, gath, mask, part_sum, relay, ring_in, full, cut_sum, last_in):
        self.at, self.copies, self.key_ref, self.mx_ref = at, copies, key_ref, mx_ref
        self.cs, self.gath, self.mask, self.part_sum, self.relay = cs, gath, mask, part_sum, relay
        self.ring_in, self.full, self.cut_sum, self.last_in = ring_in, full, cut_sum, last_in
        self.me = [at[dims[0]] * 2 + at["c"] for dims in PARTS]
        self.gather_rows = (pl.ds(0, CUT), pl.ds(CUT, SLAB - CUT))
        self.sum_rows = (pl.ds(0, 512), pl.ds(512, 512))

    def toward(self, p, k, by):
        return moved(self.at, PARTS[p][k], by)

    def arrived(self, p, *indices):
        self.copies.arrived(*[p * PER_PART + k for k in indices])

    def send(self, p, index, src, dst, there):
        self.copies.start(p * PER_PART + index, src, dst, there)

    def open(self, p):
        own, mate = self.gath.at[p, self.me[p]], moved(self.at, "c", 1)
        low, high = self.gather_rows
        self.gath[p, self.me[p], 0:16, :] = self.key_ref[p]
        self.gath[p, self.me[p], 16:SLAB, :] = self.cs[p * 1024 : (p + 1) * 1024, :].astype(BF16)
        self.send(p, 0, own.at[low], own.at[low], self.toward(p, 0, 1))
        self.send(p, 3, own.at[low], own.at[low], self.toward(p, 0, 3))
        self.send(p, 2, own.at[high], own.at[high], self.toward(p, 0, 3))
        self.send(p, 4, own, own, mate)

    def pass_on(self, p, half, step, index, there):
        slot = lax.rem(self.at[PARTS[p][0]] + step, RING) * 2 + self.at["c"]
        ref = self.gath.at[p, slot, self.gather_rows[half]]
        self.send(p, index, ref, ref, there)

    def low_first(self, p):
        mate, nxt = moved(self.at, "c", 1), self.toward(p, 0, 1)
        own, high = self.gath.at[p, self.me[p]], self.gather_rows[1]
        self.arrived(p, 0)
        self.pass_on(p, 0, 3, 5, nxt)
        self.send(p, 1, own.at[high], own.at[high], nxt)
        self.pass_on(p, 0, 3, 6, mate)

    def low_second(self, p):
        self.arrived(p, 3)
        self.pass_on(p, 0, 1, 10, moved(self.at, "c", 1))

    def high_first(self, p):
        mate, prv = moved(self.at, "c", 1), self.toward(p, 0, 3)
        self.arrived(p, 2)
        self.pass_on(p, 1, 1, 7, prv)
        self.pass_on(p, 1, 1, 8, mate)

    def low_third(self, p):
        self.arrived(p, 5)
        self.pass_on(p, 0, 2, 11, moved(self.at, "c", 1))

    def high_rest(self, p):
        mate = moved(self.at, "c", 1)
        self.arrived(p, 1)
        self.pass_on(p, 1, 3, 9, mate)
        self.arrived(p, 7)
        self.pass_on(p, 1, 2, 12, mate)

    def build_mask(self, p):
        gath, mask = self.gath, self.mask
        lane = lax.broadcasted_iota(jnp.int32, (1, 128), 1)
        rows = lax.broadcasted_iota(jnp.int32, (256, 128), 0).astype(F32)
        mine = self.me[p].astype(F32)
        for a in range(RING):
            k0 = gath[p, 2 * a, 0:16, :].astype(F32)
            k1 = gath[p, 2 * a + 1, 0:16, :].astype(F32)
            high_key = jnp.where(lane < ITEMS, k0[0:1, :], k1[0:1, :])
            low_key = jnp.where(lane < ITEMS, k0[8:9, :], k1[8:9, :])
            key = jnp.where(high_key == mine, low_key, -1.0)
            mask[p, :, a * 128 : (a + 1) * 128] = jnp.where(rows == key, 1.0, 0.0).astype(BF16)

    def add_up(self, p, half):
        gath, part_sum = self.gath, self.part_sum
        if half == 0:
            self.arrived(p, 4, 6, 10, 11)
            self.build_mask(p)
        else:
            self.arrived(p, 8, 9, 12)

        @pl.loop(0, 2)
        def _(twice):
            for inner in range(2):
                pair = half * 4 + twice * 2 + inner

                def level(fl):
                    start = pl.multiple_of(16 + fl * ITEMS, 16)
                    return jnp.concatenate([gath[p, s, pl.ds(start, ITEMS), :] for s in range(8)], axis=0)

                rhs = jnp.concatenate([level(2 * pair), level(2 * pair + 1)], axis=1)
                out = jnp.dot(self.mask[p], rhs, preferred_element_type=F32).astype(BF16)
                for side in range(2):
                    start = pl.multiple_of((2 * pair + side) * 64, 64)
                    for b in range(RING):
                        part_sum[p, b, pl.ds(start, 64), :] = out[b * 64 : (b + 1) * 64, side * 128 : (side + 1) * 128]

        nxt, prv = self.toward(p, 1, 1), self.toward(p, 1, 3)
        dim = PARTS[p][1]
        far, rows = lax.rem(self.at[dim] + 2, RING), self.sum_rows[half]
        if half == 0:
            self.send(p, 13, part_sum.at[p, far, rows], self.relay.at[p, 0], nxt)
            self.send(p, 16, part_sum.at[p, prv[dim], rows], self.ring_in.at[p, 1, rows], prv)
        else:
            self.send(p, 14, part_sum.at[p, far, rows], self.relay.at[p, 1], prv)
            self.send(p, 15, part_sum.at[p, nxt[dim], rows], self.ring_in.at[p, 0, rows], nxt)

    def ring_on(self, p, half):
        there = self.toward(p, 1, 3 if half else 1)
        to, rows = there[PARTS[p][1]], self.sum_rows[half]
        self.arrived(p, 13 + half)
        total = self.part_sum[p, to, rows, :].astype(F32) + self.relay[p, half].astype(F32)
        self.part_sum[p, to, rows, :] = total.astype(BF16)
        self.send(p, 17 + half, self.part_sum.at[p, to, rows], self.ring_in.at[p, half, rows], there)

    def ring_end(self, p, half):
        part_sum, ring_in, full, cut_sum = self.part_sum, self.ring_in, self.full, self.cut_sum
        if half == 0:
            self.arrived(p, 16, 17)
        else:
            self.arrived(p, 15, 18)
        own = self.at[PARTS[p][1]]

        @pl.loop(0, 4)
        def _(quad):
            for inner in range(2):
                fl = half * 8 + quad * 2 + inner
                block = pl.ds(pl.multiple_of(fl * 64, 64), 64)
                total = part_sum[p, own, block, :].astype(F32) + ring_in[p, 0, block, :].astype(F32) + ring_in[p, 1, block, :].astype(F32)
                full[p, block, :] = total
                narrow = total.astype(BF16)
                for c in range(RING):
                    cut_sum[p, c, pl.ds(pl.multiple_of(fl * 16, 16), 16), :] = narrow[c * 16 : (c + 1) * 16, :]

        rows = pl.ds(half * 128, 128)
        for k, by in enumerate((1, 3, 2)):
            there = self.toward(p, 2, by)
            self.send(p, 19 + half * 3 + k, cut_sum.at[p, there[PARTS[p][2]], rows], self.last_in.at[p, k, rows], there)

    def close(self, p, half):
        self.arrived(p, *[19 + half * 3 + k for k in range(3)])
        for fl in range(half * 8, half * 8 + 8):
            start = pl.multiple_of(fl * 64 + self.at[PARTS[p][2]] * 16, 16)
            here = slice(fl * 16, fl * 16 + 16)
            total = self.full[p, pl.ds(start, 16), :]
            for k in range(3):
                total = total + self.last_in[p, k, here, :].astype(F32)
            self.mx_ref[p * 256 + fl * 16 : p * 256 + fl * 16 + 16, :] = total


def contributions(met_ref, weight_ref, cs):
    @pl.loop(0, ITEMS // 4)
    def _(group):
        for k in range(4):
            s = group * 4 + k
            cs[pl.ds(s, 48, stride=ITEMS), :] = jnp.dot(met_ref[s], weight_ref[s], preferred_element_type=F32)


def greet(at, near):
    barrier = pltpu.get_barrier_semaphore()
    peers = [moved(at, dim, by) for dim in ("x", "y", "z") for by in (1, 2, 3)] + [moved(at, "c", 1)]
    peers = [device(there) for there in peers] + [near[side] for side in "nsew"]
    for there in peers:
        pl.semaphore_signal(barrier, inc=1, device_id=there, device_id_type=MESH)
    return barrier, len(peers)


REGRID_SCRATCH = [
    pltpu.VMEM((48 * ITEMS, 128), F32),
    pltpu.VMEM((3, 8, SLAB, 128), BF16),
    pltpu.VMEM((3, 256, 512), BF16),
    pltpu.VMEM((3, RING, 1024, 128), BF16),
    pltpu.VMEM((3, 2, 512, 128), BF16),
    pltpu.VMEM((3, 2, 1024, 128), BF16),
    pltpu.VMEM((3, 1024, 128), F32),
    pltpu.VMEM((3, RING, 256, 128), BF16),
    pltpu.VMEM((3, 3, 256, 128), BF16),
]


def keys_of(block_dest, block_row):
    face, tile = block_dest >> 4, block_dest & 15
    pos = {"x": tile & 3, "y": face >> 1, "z": tile >> 2}
    out = []
    for first, second, third in PARTS:
        high = pos[first] * 2 + (face & 1)
        low = pos[second] * 64 + pos[third] * 16 + block_row
        both = jnp.stack([high, low])[:, None, :]
        both = jnp.broadcast_to(both, (2, 8, ITEMS)).reshape(16, ITEMS)
        out.append(jnp.concatenate([both, both], axis=1))
    return jnp.stack(out).astype(BF16)


SPECIES = 256
UNROLL = 4
HALO_COPIES = 75


def lanes_of(shape, dim):
    return lax.broadcasted_iota(jnp.int32, shape, dim)


def edge_picker(pick):
    row, lane = lanes_of((128, 128), 0), lanes_of((128, 128), 1)
    for r in range(16):
        east = jnp.logical_and(row == 127, lane == 2 * r)
        west = jnp.logical_and(row == 0, lane == 2 * r + 1)
        pick[r * 128 : (r + 1) * 128, :] = jnp.where(jnp.logical_or(east, west), 1.0, 0.0).astype(BF16)


def picked_edges(narrow, pick, l):
    rows = jnp.concatenate([narrow[l, r] for r in range(16)], axis=1)
    return jnp.dot(rows, pick[...], preferred_element_type=F32).astype(BF16)


def neighbours():
    face, tile = lax.axis_index("face"), lax.axis_index("tile")
    return {
        "n": (lax.rem(face + 1, 8), tile),
        "s": (lax.rem(face + 7, 8), tile),
        "e": (face, lax.rem(tile + 1, 16)),
        "w": (face, lax.rem(tile + 15, 16)),
    }


def start_tracers(tracer_ref, amount, load):
    count = tracer_ref.shape[0]
    copies = []
    for lr in range(64):
        copy = pltpu.make_async_copy(
            tracer_ref.at[:, lr, 0], amount.at[lr // 16, lr % 16 + 1, pl.ds(0, count)], load.at[lr]
        )
        copy.start()
        copies.append(copy)
    return copies


def first_rows(near, copies, loads, amount, narrow, row_in):
    for copy in loads:
        copy.wait()

    @pl.loop(0, 64)
    def _(lr):
        narrow[lr // 16, lax.rem(lr, 16)] = amount[lr // 16, lax.rem(lr, 16) + 1].astype(BF16)

    copies.start(HALO_COPIES + 0, narrow.at[:, 15], row_in.at[0, 0], near["n"])
    copies.start(HALO_COPIES + 1, narrow.at[:, 0], row_in.at[0, 1], near["s"])


def first_columns(near, copies, narrow, pick, edges, edge_in):
    @pl.loop(0, 4)
    def _(l):
        edges[0, l] = picked_edges(narrow, pick, l)

    copies.start(HALO_COPIES + 2, edges.at[0], edge_in.at[0, 0], near["e"])
    copies.start(HALO_COPIES + 3, edges.at[0], edge_in.at[0, 1], near["w"])


def send_courant(near, copies, mx_ref, courant, courant_in):
    courant[0] = 0.3 * jnp.tanh(mx_ref[0:64, :])
    courant[1] = 0.3 * jnp.tanh(mx_ref[64:128, :])
    copies.start(HALO_COPIES + 4, courant.at[0], courant_in.at[0], near["n"])
    copies.start(HALO_COPIES + 5, courant.at[1], courant_in.at[1], near["e"])


def light_of(mx_ref):
    depth = jnp.zeros((16, 128), F32)
    for l in range(4):
        value = mx_ref[128 + l * 16 : 144 + l * 16, :]
        depth = depth + (jnp.maximum(value, 0.0) + jnp.log1p(jnp.exp(-jnp.abs(value))))
        mx_ref[768 + l * 16 : 784 + l * 16, :] = jnp.exp(-depth)
    mx_ref[832:1024, :] = jnp.zeros((192, 128), F32)


def coefficients(copies, courant, courant_in, shifted, coef, band):
    row, lane = lanes_of((128, 128), 0), lanes_of((128, 128), 1)
    from_west = jnp.where(row == lane - 1, 1.0, 0.0)
    from_east = jnp.where(row == lane + 1, 1.0, 0.0)
    sub, edge = lanes_of((16, 128), 0), lanes_of((16, 128), 1)
    copies.arrived(HALO_COPIES + 4, HALO_COPIES + 5)
    for l in range(4):
        rows = slice(l * 16, l * 16 + 16)
        shifted[l, 8:24, :] = courant[0, rows, :]
        shifted[l, 7:8, :] = courant_in[0, l * 16 + 15 : l * 16 + 16, :]
        cx, cy = courant[0, rows, :], courant[1, rows, :]
        behind_x = shifted[l, 7:23, :]
        behind_y = jnp.where(edge == 0, pltpu.roll(courant_in[1, rows, :], 1, 1), pltpu.roll(cy, 1, 1))
        coef[l, 0] = 1.0 - jnp.maximum(cx, 0.0) + jnp.minimum(behind_x, 0.0) - jnp.maximum(cy, 0.0) + jnp.minimum(behind_y, 0.0)
        coef[l, 1] = jnp.maximum(behind_x, 0.0)
        coef[l, 2] = -jnp.minimum(cx, 0.0)
        west, east = jnp.maximum(behind_y, 0.0), -jnp.minimum(cy, 0.0)
        for r in range(16):
            w, e = west[r : r + 1, :], east[r : r + 1, :]
            band[l, r, 0:128, :] = (from_west * w + from_east * e).astype(BF16)
            k = 2 * r % 16
            ends = jnp.where(jnp.logical_and(sub == k, edge == 0), w, jnp.where(jnp.logical_and(sub == k + 1, edge == 127), e, 0.0))
            other = 128 + 16 * (1 - r // 8)
            band[l, r, 128 + 16 * (r // 8) : 144 + 16 * (r // 8), :] = ends.astype(BF16)
            band[l, r, other : other + 16, :] = jnp.zeros((16, 128), BF16)


def advance(source, target, narrow, side, coef, band, row_in, edge_in, step, l, keep):
    source[l, 0] = row_in[step, 0, l].astype(F32)
    source[l, 17] = row_in[step, 1, l].astype(F32)
    even = lax.rem(lanes_of((SPECIES, 128), 1), 2) == 0
    side[...] = jnp.where(even, edge_in[step, 0, l].astype(F32), edge_in[step, 1, l].astype(F32)).astype(BF16)

    @pl.loop(0, 16 // UNROLL)
    def _(group):
        across = []
        for k in range(UNROLL):
            r = group * UNROLL + k
            lhs = jnp.concatenate([narrow[l, r], side[...]], axis=1)
            across.append(jnp.dot(lhs, band[l, r], preferred_element_type=F32))
        for k in range(UNROLL):
            r = group * UNROLL + k
            total = coef[l, 0, pl.ds(r, 1), :] * source[l, r + 1] + coef[l, 1, pl.ds(r, 1), :] * source[l, r]
            total = total + coef[l, 2, pl.ds(r, 1), :] * source[l, r + 2] + across[k]
            target[l, r + 1] = total
            if keep:
                narrow[l, r] = total.astype(BF16)


def first_step(near, copies, l, amount, middle, narrow, side, pick, edges, coef, band, row_in, edge_in):
    if l == 0:
        copies.arrived(*[HALO_COPIES + k for k in range(4)])
        copies.sent_of(HALO_COPIES + 0, HALO_COPIES + 1)
    advance(amount, middle, narrow, side, coef, band, row_in, edge_in, 0, l, True)
    base = HALO_COPIES + 6 + 4 * l
    copies.start(base + 0, narrow.at[l, 15], row_in.at[1, 0, l], near["n"])
    copies.start(base + 1, narrow.at[l, 0], row_in.at[1, 1, l], near["s"])
    edges[1, l] = picked_edges(narrow, pick, l)
    copies.start(base + 2, edges.at[1, l], edge_in.at[1, 0, l], near["e"])
    copies.start(base + 3, edges.at[1, l], edge_in.at[1, 1, l], near["w"])


def second_step(copies, l, adv_ref, amount, middle, narrow, side, coef, band, row_in, edge_in, store):
    base = HALO_COPIES + 6 + 4 * l
    copies.arrived(*[base + k for k in range(4)])
    advance(middle, amount, narrow, side, coef, band, row_in, edge_in, 1, l, False)
    copy = pltpu.make_async_copy(amount.at[l, pl.ds(1, 16)], adv_ref.at[l], store.at[l])
    copy.start()
    return copy


ADVECT_SCRATCH = [
    pltpu.VMEM((4, 18, SPECIES, 128), F32),
    pltpu.VMEM((4, 18, SPECIES, 128), F32),
    pltpu.VMEM((4, 16, SPECIES, 128), BF16),
    pltpu.VMEM((SPECIES, 128), BF16),
    pltpu.VMEM((2048, 128), BF16),
    pltpu.VMEM((2, 4, SPECIES, 128), BF16),
    pltpu.VMEM((2, 2, 4, SPECIES, 128), BF16),
    pltpu.VMEM((2, 2, 4, SPECIES, 128), BF16),
    pltpu.VMEM((2, 64, 128), F32),
    pltpu.VMEM((2, 64, 128), F32),
    pltpu.VMEM((4, 24, 128), F32),
    pltpu.VMEM((4, 3, 16, 128), F32),
    pltpu.VMEM((4, 16, 256, 128), BF16),
]
COPIES = HALO_COPIES + 22


def transport_kernel(met_ref, weight_ref, key_ref, tracer_ref, mx_ref, adv_ref, send, recv, load, store, *scratch):
    cut = len(REGRID_SCRATCH)
    regrid_scratch = scratch[:cut]
    amount, middle, narrow, side, pick, edges, row_in, edge_in, courant, courant_in, shifted, coef, band = scratch[cut:]
    at, near = whereabouts(), neighbours()
    loads = start_tracers(tracer_ref, amount, load)
    barrier, count = greet(at, near)
    contributions(met_ref, weight_ref, regrid_scratch[0])
    pl.semaphore_wait(barrier, count)
    copies = Copies(send, recv)

    flow = Regrid(at, copies, key_ref, mx_ref, *regrid_scratch)
    every = range(3)
    for p in every:
        flow.open(p)

    edge_picker(pick)

    @pl.loop(0, 64)
    def _(k):
        band[k // 16, lax.rem(k, 16), 128:256, :] = jnp.zeros((128, 128), BF16)

    for p in every:
        flow.low_first(p)
        flow.low_second(p)
    first_rows(near, copies, loads, amount, narrow, row_in)
    for p in every:
        flow.high_first(p)
    first_columns(near, copies, narrow, pick, edges, edge_in)
    for p in every:
        flow.low_third(p)
    for p in every:
        flow.add_up(p, 0)
    for p in every:
        flow.high_rest(p)
    for p in every:
        flow.ring_on(p, 0)
    flow.add_up(0, 1)
    flow.ring_end(0, 0)
    flow.add_up(1, 1)
    flow.add_up(2, 1)
    for p in every:
        flow.ring_on(p, 1)
    flow.close(0, 0)
    send_courant(near, copies, mx_ref, courant, courant_in)
    flow.ring_end(1, 0)
    flow.ring_end(2, 0)
    coefficients(copies, courant, courant_in, shifted, coef, band)
    first = (amount, middle, narrow, side, pick, edges, coef, band, row_in, edge_in)
    second = (adv_ref, amount, middle, narrow, side, coef, band, row_in, edge_in, store)
    flow.ring_end(0, 1)
    first_step(near, copies, 0, *first)
    flow.ring_end(1, 1)
    flow.ring_end(2, 1)
    for l in range(1, 4):
        first_step(near, copies, l, *first)
    stores = [second_step(copies, l, *second) for l in range(4)]
    flow.close(0, 1)
    light_of(mx_ref)
    for p in (1, 2):
        for half in range(2):
            flow.close(p, half)
    for copy in stores:
        copy.wait()
    copies.sent()


def transport_call(met_src, weights, keys, tracers):
    vmem, anywhere = pl.BlockSpec(memory_space=pltpu.VMEM), pl.BlockSpec(memory_space=pl.ANY)
    dma = pltpu.SemaphoreType.DMA
    return pl.pallas_call(
        transport_kernel,
        out_shape=(jax.ShapeDtypeStruct((1024, 128), F32), jax.ShapeDtypeStruct((4, 16, SPECIES, 128), F32)),
        in_specs=[vmem] * 3 + [anywhere],
        out_specs=(vmem, anywhere),
        scratch_shapes=[dma((COPIES,)), dma((COPIES,)), dma((64,)), dma((4,))] + REGRID_SCRATCH + ADVECT_SCRATCH,
        compiler_params=pltpu.CompilerParams(collective_id=0, has_side_effects=True, vmem_limit_bytes=60 << 20),
        name="transport",
    )(met_src, weights, keys, tracers)


CHUNK = 4


def chemistry_kernel(mx_ref, rate_ref, adv_ref, met_ref, out_ref, amount, result, load, store):
    chunks = 64 // CHUNK
    count = out_ref.shape[0]

    def fetch(k):
        rows = pl.ds(k * CHUNK, CHUNK)
        return pltpu.make_async_copy(adv_ref.at[rows], amount.at[rows], load.at[k])

    def put(lr):
        return pltpu.make_async_copy(result.at[lr, pl.ds(0, count)], out_ref.at[:, lr, 0], store.at[lr])

    for k in range(chunks):
        fetch(k).start()
    met_ref[...] = mx_ref[0:768, :]

    def fields(lr):
        value = mx_ref[pl.ds(lr, 16, stride=64), :]
        m1 = value.astype(BF16)
        rest = value - m1.astype(F32)
        m2 = rest.astype(BF16)
        m3 = (rest - m2.astype(F32)).astype(BF16)
        return jnp.concatenate([m1, m2, m3, m1, m2, m1], axis=0)

    @pl.loop(0, chunks)
    def _(k):
        fetch(k).wait()
        for pair in range(CHUNK // 2):
            lr = k * CHUNK + 2 * pair
            rhs = jnp.concatenate([fields(lr), fields(lr + 1)], axis=1)
            exponent = jnp.dot(rate_ref[...], rhs, preferred_element_type=F32)
            loss = jnp.maximum(exponent, 0.0) + jnp.log(1.0 + jnp.exp(-jnp.abs(exponent)))
            for side in range(2):
                result[lr + side] = amount[lr + side] / (1.0 + loss[:, side * 128 : side * 128 + 128])
                put(lr + side).start()

    @pl.loop(0, 64)
    def _(lr):
        put(lr).wait()


def chemistry_call(mx, rates, adv, count):
    vmem, anywhere = pl.BlockSpec(memory_space=pltpu.VMEM), pl.BlockSpec(memory_space=pl.ANY)
    dma = pltpu.SemaphoreType.DMA
    return pl.pallas_call(
        chemistry_kernel,
        out_shape=(jax.ShapeDtypeStruct((768, 128), F32), jax.ShapeDtypeStruct((count, 64, 1, 128), F32)),
        in_specs=[vmem, vmem, anywhere],
        out_specs=(vmem, anywhere),
        scratch_shapes=[pltpu.VMEM((64, SPECIES, 128), F32), pltpu.VMEM((64, SPECIES, 128), F32), dma((64 // CHUNK,)), dma((64,))],
        compiler_params=pltpu.CompilerParams(vmem_limit_bytes=62 << 20),
        name="chemistry",
    )(mx, rates, adv)


def rates_of(rate_coef, photo_coef):
    both = jnp.concatenate([rate_coef, photo_coef[:, None]], axis=1)
    both = jnp.pad(both, ((0, SPECIES - both.shape[0]), (0, 16 - both.shape[1])))
    r1 = lax.reduce_precision(both, 8, 7)
    r2 = lax.reduce_precision(both - r1, 8, 7)
    r3 = both - r1 - r2
    return jnp.concatenate([r1, r1, r1, r2, r2, r3], axis=1).astype(BF16)


def local(met_src, intersection_weights, block_dest, block_row, tracers, rate_coef, photo_coef):
    species, levels, rows, cells = tracers.shape
    keys = keys_of(block_dest, block_row)
    rates = rates_of(rate_coef, photo_coef)
    mx, adv = transport_call(met_src, intersection_weights, keys, tracers.reshape(species, levels * rows, 1, cells))
    met, out = chemistry_call(mx, rates, adv.reshape(levels * rows, SPECIES, cells), species)
    return met.reshape(-1, levels, rows, cells), out.reshape(species, levels, rows, cells)


def solution(mesh):
    split = P(("face", "tile"))
    grid = P(None, None, "face", "tile")
    return jax.shard_map(
        local,
        mesh=mesh,
        in_specs=(split, split, split, split, grid, P(), P()),
        out_specs=(grid, grid),
        check_vma=False,
    )
```

```python
import functools
import jax
import jax.numpy as jnp
from jax import lax
from jax.experimental import pallas as pl
from jax.experimental.pallas import tpu as pltpu
from jax.sharding import PartitionSpec as P

MESH = pl.DeviceIdType.MESH
F32 = jnp.float32
BF16 = jnp.bfloat16
PARTS = (("x", "y", "z"), ("y", "z", "x"), ("z", "x", "y"))
RING = 4
ITEMS = 64
SLAB = 16 + 16 * ITEMS
CUT = 16 + 8 * ITEMS
PER_PART = 25


def whereabouts():
    face = lax.axis_index("face")
    tile = lax.axis_index("tile")
    return {"x": lax.rem(tile, 4), "y": face // 2, "z": tile // 4, "c": lax.rem(face, 2)}


def device(at):
    return (at["y"] * 2 + at["c"], at["z"] * 4 + at["x"])


def moved(at, dim, by):
    there = dict(at)
    there[dim] = 1 - at[dim] if dim == "c" else lax.rem(at[dim] + by, RING)
    return there


class Copies:
    def __init__(self, send, recv):
        self.send, self.recv, self.made, self.over = send, recv, {}, set()

    def start(self, index, src, dst, there):
        copy = pltpu.make_async_remote_copy(
            src_ref=src,
            dst_ref=dst,
            send_sem=self.send.at[index],
            recv_sem=self.recv.at[index],
            device_id=device(there) if isinstance(there, dict) else there,
            device_id_type=MESH,
        )
        copy.start()
        self.made[index] = copy

    def arrived(self, *indices):
        for index in indices:
            self.made[index].wait_recv()

    def sent_of(self, *indices):
        for index in indices:
            self.made[index].wait_send()
            self.over.add(index)

    def sent(self):
        self.sent_of(*[index for index in self.made if index not in self.over])


class Regrid:
    def __init__(self, at, copies, key_ref, mx_ref, cs, gath, mask, part_sum, relay, ring_in, full, cut_sum, last_in):
        self.at, self.copies, self.key_ref, self.mx_ref = at, copies, key_ref, mx_ref
        self.cs, self.gath, self.mask, self.part_sum, self.relay = cs, gath, mask, part_sum, relay
        self.ring_in, self.full, self.cut_sum, self.last_in = ring_in, full, cut_sum, last_in
        self.me = [at[dims[0]] * 2 + at["c"] for dims in PARTS]
        self.gather_rows = (pl.ds(0, CUT), pl.ds(CUT, SLAB - CUT))
        self.sum_rows = (pl.ds(0, 512), pl.ds(512, 512))

    def toward(self, p, k, by):
        return moved(self.at, PARTS[p][k], by)

    def arrived(self, p, *indices):
        self.copies.arrived(*[p * PER_PART + k for k in indices])

    def send(self, p, index, src, dst, there):
        self.copies.start(p * PER_PART + index, src, dst, there)

    def open(self, p):
        own, mate = self.gath.at[p, self.me[p]], moved(self.at, "c", 1)
        low, high = self.gather_rows
        self.gath[p, self.me[p], 0:16, :] = self.key_ref[p]
        self.gath[p, self.me[p], 16:SLAB, :] = self.cs[p * 1024 : (p + 1) * 1024, :].astype(BF16)
        self.send(p, 0, own.at[low], own.at[low], self.toward(p, 0, 1))
        self.send(p, 3, own.at[low], own.at[low], self.toward(p, 0, 3))
        self.send(p, 2, own.at[high], own.at[high], self.toward(p, 0, 3))
        self.send(p, 4, own, own, mate)

    def pass_on(self, p, half, step, index, there):
        slot = lax.rem(self.at[PARTS[p][0]] + step, RING) * 2 + self.at["c"]
        ref = self.gath.at[p, slot, self.gather_rows[half]]
        self.send(p, index, ref, ref, there)

    def low_first(self, p):
        mate, nxt = moved(self.at, "c", 1), self.toward(p, 0, 1)
        own, high = self.gath.at[p, self.me[p]], self.gather_rows[1]
        self.arrived(p, 0)
        self.pass_on(p, 0, 3, 5, nxt)
        self.send(p, 1, own.at[high], own.at[high], nxt)
        self.pass_on(p, 0, 3, 6, mate)

    def low_second(self, p):
        self.arrived(p, 3)
        self.pass_on(p, 0, 1, 10, moved(self.at, "c", 1))

    def high_first(self, p):
        mate, prv = moved(self.at, "c", 1), self.toward(p, 0, 3)
        self.arrived(p, 2)
        self.pass_on(p, 1, 1, 7, prv)
        self.pass_on(p, 1, 1, 8, mate)

    def low_third(self, p):
        self.arrived(p, 5)
        self.pass_on(p, 0, 2, 11, moved(self.at, "c", 1))

    def high_rest(self, p):
        mate = moved(self.at, "c", 1)
        self.arrived(p, 1)
        self.pass_on(p, 1, 3, 9, mate)
        self.arrived(p, 7)
        self.pass_on(p, 1, 2, 12, mate)

    def build_mask(self, p):
        gath, mask = self.gath, self.mask
        lane = lax.broadcasted_iota(jnp.int32, (1, 128), 1)
        rows = lax.broadcasted_iota(jnp.int32, (256, 128), 0).astype(F32)
        mine = self.me[p].astype(F32)
        for a in range(RING):
            k0 = gath[p, 2 * a, 0:16, :].astype(F32)
            k1 = gath[p, 2 * a + 1, 0:16, :].astype(F32)
            high_key = jnp.where(lane < ITEMS, k0[0:1, :], k1[0:1, :])
            low_key = jnp.where(lane < ITEMS, k0[8:9, :], k1[8:9, :])
            key = jnp.where(high_key == mine, low_key, -1.0)
            mask[p, :, a * 128 : (a + 1) * 128] = jnp.where(rows == key, 1.0, 0.0).astype(BF16)

    def add_up(self, p, half):
        gath, part_sum = self.gath, self.part_sum
        if half == 0:
            self.arrived(p, 4, 6, 10, 11)
            self.build_mask(p)
        else:
            self.arrived(p, 8, 9, 12)

        @pl.loop(0, 2)
        def _(twice):
            for inner in range(2):
                pair = half * 4 + twice * 2 + inner

                def level(fl):
                    start = pl.multiple_of(16 + fl * ITEMS, 16)
                    return jnp.concatenate([gath[p, s, pl.ds(start, ITEMS), :] for s in range(8)], axis=0)

                rhs = jnp.concatenate([level(2 * pair), level(2 * pair + 1)], axis=1)
                out = jnp.dot(self.mask[p], rhs, preferred_element_type=F32).astype(BF16)
                for side in range(2):
                    start = pl.multiple_of((2 * pair + side) * 64, 64)
                    for b in range(RING):
                        part_sum[p, b, pl.ds(start, 64), :] = out[b * 64 : (b + 1) * 64, side * 128 : (side + 1) * 128]

        nxt, prv = self.toward(p, 1, 1), self.toward(p, 1, 3)
        dim = PARTS[p][1]
        far, rows = lax.rem(self.at[dim] + 2, RING), self.sum_rows[half]
        if half == 0:
            self.send(p, 13, part_sum.at[p, far, rows], self.relay.at[p, 0], nxt)
            self.send(p, 16, part_sum.at[p, prv[dim], rows], self.ring_in.at[p, 1, rows], prv)
        else:
            self.send(p, 14, part_sum.at[p, far, rows], self.relay.at[p, 1], prv)
            self.send(p, 15, part_sum.at[p, nxt[dim], rows], self.ring_in.at[p, 0, rows], nxt)

    def ring_on(self, p, half):
        there = self.toward(p, 1, 3 if half else 1)
        to, rows = there[PARTS[p][1]], self.sum_rows[half]
        self.arrived(p, 13 + half)
        total = self.part_sum[p, to, rows, :].astype(F32) + self.relay[p, half].astype(F32)
        self.part_sum[p, to, rows, :] = total.astype(BF16)
        self.send(p, 17 + half, self.part_sum.at[p, to, rows], self.ring_in.at[p, half, rows], there)

    def ring_end(self, p, half):
        part_sum, ring_in, full, cut_sum = self.part_sum, self.ring_in, self.full, self.cut_sum
        if half == 0:
            self.arrived(p, 16, 17)
        else:
            self.arrived(p, 15, 18)
        own = self.at[PARTS[p][1]]

        @pl.loop(0, 4)
        def _(quad):
            for inner in range(2):
                fl = half * 8 + quad * 2 + inner
                block = pl.ds(pl.multiple_of(fl * 64, 64), 64)
                total = part_sum[p, own, block, :].astype(F32) + ring_in[p, 0, block, :].astype(F32) + ring_in[p, 1, block, :].astype(F32)
                full[p, block, :] = total
                narrow = total.astype(BF16)
                for c in range(RING):
                    cut_sum[p, c, pl.ds(pl.multiple_of(fl * 16, 16), 16), :] = narrow[c * 16 : (c + 1) * 16, :]

        rows = pl.ds(half * 128, 128)
        for k, by in enumerate((1, 3, 2)):
            there = self.toward(p, 2, by)
            self.send(p, 19 + half * 3 + k, cut_sum.at[p, there[PARTS[p][2]], rows], self.last_in.at[p, k, rows], there)

    def close(self, p, half):
        self.arrived(p, *[19 + half * 3 + k for k in range(3)])
        for fl in range(half * 8, half * 8 + 8):
            start = pl.multiple_of(fl * 64 + self.at[PARTS[p][2]] * 16, 16)
            here = slice(fl * 16, fl * 16 + 16)
            total = self.full[p, pl.ds(start, 16), :]
            for k in range(3):
                total = total + self.last_in[p, k, here, :].astype(F32)
            self.mx_ref[p * 256 + fl * 16 : p * 256 + fl * 16 + 16, :] = total


def contributions(met_ref, weight_ref, cs, part):
    @pl.loop(0, ITEMS // 16)
    def _(group):
        for k in range(4):
            s = part * (ITEMS // 4) + group * 4 + k
            cs[pl.ds(s, 48, stride=ITEMS), :] = jnp.dot(met_ref[s], weight_ref[s], preferred_element_type=F32)


def greet(at, near):
    barrier = pltpu.get_barrier_semaphore()
    peers = [moved(at, dim, by) for dim in ("x", "y", "z") for by in (1, 2, 3)] + [moved(at, "c", 1)]
    peers = [device(there) for there in peers] + [near[side] for side in "nsew"]
    for there in peers:
        pl.semaphore_signal(barrier, inc=1, device_id=there, device_id_type=MESH)
    return barrier, len(peers)


REGRID_SCRATCH = [
    pltpu.VMEM((48 * ITEMS, 128), F32),
    pltpu.VMEM((3, 8, SLAB, 128), BF16),
    pltpu.VMEM((3, 256, 512), BF16),
    pltpu.VMEM((3, RING, 1024, 128), BF16),
    pltpu.VMEM((3, 2, 512, 128), BF16),
    pltpu.VMEM((3, 2, 1024, 128), BF16),
    pltpu.VMEM((3, 1024, 128), F32),
    pltpu.VMEM((3, RING, 256, 128), BF16),
    pltpu.VMEM((3, 3, 256, 128), BF16),
]


def keys_of(dest, row):
    dest, row = jnp.concatenate([dest, dest], axis=1), jnp.concatenate([row, row], axis=1)
    face, tile = dest >> 4, dest & 15
    pos = {"x": tile & 3, "y": face >> 1, "z": tile >> 2}
    upper = lax.broadcasted_iota(jnp.int32, (16, 128), 0) < 8
    out = []
    for first, second, third in PARTS:
        high = pos[first] * 2 + (face & 1)
        low = pos[second] * 64 + pos[third] * 16 + row
        out.append(jnp.where(upper, high.astype(F32), low.astype(F32)).astype(BF16))
    return out


SPECIES = 256
UNROLL = 4
HALO_COPIES = 75


def lanes_of(shape, dim):
    return lax.broadcasted_iota(jnp.int32, shape, dim)


def edge_picker(pick):
    row, lane = lanes_of((128, 128), 0), lanes_of((128, 128), 1)

    @pl.loop(0, 64)
    def _(lr):
        east = jnp.logical_and(row == 127, lane == 2 * lr)
        west = jnp.logical_and(row == 0, lane == 2 * lr + 1)
        pick[pl.ds(pl.multiple_of(lr * 128, 128), 128), :] = jnp.where(jnp.logical_or(east, west), 1.0, 0.0).astype(BF16)


def picked_edges(narrow, pick, l):
    rows = jnp.concatenate([narrow[l, r] for r in range(16)], axis=1)
    start = l * 2048 if isinstance(l, int) else pl.multiple_of(l * 2048, 2048)
    return jnp.dot(rows, pick[pl.ds(start, 2048), :], preferred_element_type=F32)


def neighbours():
    face, tile = lax.axis_index("face"), lax.axis_index("tile")
    return {
        "n": (lax.rem(face + 1, 8), tile),
        "s": (lax.rem(face + 7, 8), tile),
        "e": (face, lax.rem(tile + 1, 16)),
        "w": (face, lax.rem(tile + 15, 16)),
    }


def start_tracers(tracer_ref, amount, load):
    count = tracer_ref.shape[0]
    copies = []
    for lr in range(64):
        copy = pltpu.make_async_copy(
            tracer_ref.at[:, lr, 0], amount.at[lr // 16, lr % 16 + 1, pl.ds(0, count)], load.at[lr]
        )
        copy.start()
        copies.append(copy)
    return copies


def first_rows(near, copies, loads, amount, narrow, row_in):
    for copy in loads:
        copy.wait()

    @pl.loop(0, 64)
    def _(lr):
        narrow[lr // 16, lax.rem(lr, 16)] = amount[lr // 16, lax.rem(lr, 16) + 1].astype(BF16)


def first_columns(near, copies, narrow, pick, edges, edge_in):
    edges[0] = lax.fori_loop(0, 4, lambda l, total: total + picked_edges(narrow, pick, l), jnp.zeros((SPECIES, 128), F32)).astype(BF16)


def first_sends(near, copies, narrow, edges, row_in, edge_in):
    copies.start(HALO_COPIES + 0, narrow.at[:, 15], row_in.at[0, 0], near["n"])
    copies.start(HALO_COPIES + 1, narrow.at[:, 0], row_in.at[0, 1], near["s"])
    copies.start(HALO_COPIES + 2, edges.at[0], edge_in.at[0, 0], near["e"])
    copies.start(HALO_COPIES + 3, edges.at[0], edge_in.at[0, 1], near["w"])


def send_courant(near, copies, mx_ref, courant, courant_in):
    courant[0] = 0.3 * jnp.tanh(mx_ref[0:64, :])
    courant[1] = 0.3 * jnp.tanh(mx_ref[64:128, :])
    copies.start(HALO_COPIES + 4, courant.at[0], courant_in.at[0], near["n"])
    copies.start(HALO_COPIES + 5, courant.at[1], courant_in.at[1], near["e"])


def light_of(mx_ref):
    depth = jnp.zeros((16, 128), F32)
    for l in range(4):
        value = mx_ref[128 + l * 16 : 144 + l * 16, :]
        depth = depth + (jnp.maximum(value, 0.0) + jnp.log1p(jnp.exp(-jnp.abs(value))))
        mx_ref[768 + l * 16 : 784 + l * 16, :] = jnp.exp(-depth)
    mx_ref[832:1024, :] = jnp.zeros((192, 128), F32)


def coefficients(copies, courant, courant_in, shifted, coef, band):
    row, lane = lanes_of((128, 128), 0), lanes_of((128, 128), 1)
    from_west = jnp.where(row == lane - 1, 1.0, 0.0)
    from_east = jnp.where(row == lane + 1, 1.0, 0.0)
    sub, edge = lanes_of((16, 128), 0), lanes_of((16, 128), 1)
    copies.arrived(HALO_COPIES + 4, HALO_COPIES + 5)
    for l in range(4):
        rows = slice(l * 16, l * 16 + 16)
        shifted[l, 8:24, :] = courant[0, rows, :]
        shifted[l, 7:8, :] = courant_in[0, l * 16 + 15 : l * 16 + 16, :]
        cx, cy = courant[0, rows, :], courant[1, rows, :]
        behind_x = shifted[l, 7:23, :]
        behind_y = jnp.where(edge == 0, pltpu.roll(courant_in[1, rows, :], 1, 1), pltpu.roll(cy, 1, 1))
        coef[l, 0] = 1.0 - jnp.maximum(cx, 0.0) + jnp.minimum(behind_x, 0.0) - jnp.maximum(cy, 0.0) + jnp.minimum(behind_y, 0.0)
        coef[l, 1] = jnp.maximum(behind_x, 0.0)
        coef[l, 2] = -jnp.minimum(cx, 0.0)
        west, east = jnp.maximum(behind_y, 0.0), -jnp.minimum(cy, 0.0)
        for r in range(16):
            w, e = west[r : r + 1, :], east[r : r + 1, :]
            band[l, r, 0:128, :] = (from_west * w + from_east * e).astype(BF16)
            lr = l * 16 + r
            k = 2 * lr % 16
            ends = jnp.where(jnp.logical_and(sub == k, edge == 0), w, jnp.where(jnp.logical_and(sub == k + 1, edge == 127), e, 0.0))
            band[l, r, 128 + 16 * (lr // 8) : 144 + 16 * (lr // 8), :] = ends.astype(BF16)


def advance(source, target, narrow, side, coef, band, row_in, edge_in, step, l, keep):
    source[l, 0] = row_in[step, 0, l].astype(F32)
    source[l, 17] = row_in[step, 1, l].astype(F32)
    even = lax.rem(lanes_of((SPECIES, 128), 1), 2) == 0
    if step == 0 and l == 0 or step == 1 and l % 2 == 0:
        slot = 0 if step == 0 else 1 + l // 2
        side[...] = jnp.where(even, edge_in[slot, 0].astype(F32), edge_in[slot, 1].astype(F32)).astype(BF16)

    @pl.loop(0, 16 // UNROLL)
    def _(group):
        across = []
        for k in range(UNROLL):
            r = group * UNROLL + k
            lhs = jnp.concatenate([narrow[l, r], side[...]], axis=1)
            across.append(jnp.dot(lhs, band[l, r], preferred_element_type=F32))
        for k in range(UNROLL):
            r = group * UNROLL + k
            total = coef[l, 0, pl.ds(r, 1), :] * source[l, r + 1] + coef[l, 1, pl.ds(r, 1), :] * source[l, r]
            total = total + coef[l, 2, pl.ds(r, 1), :] * source[l, r + 2] + across[k]
            target[l, r + keep] = total
            if keep:
                narrow[l, r] = total.astype(BF16)


def first_step(near, copies, l, amount, middle, narrow, side, pick, edges, coef, band, row_in, edge_in):
    if l == 0:
        copies.arrived(*[HALO_COPIES + k for k in range(4)])
        copies.sent_of(HALO_COPIES + 0, HALO_COPIES + 1)
    advance(amount, middle, narrow, side, coef, band, row_in, edge_in, 0, l, True)
    base = HALO_COPIES + 6 + 4 * l
    copies.start(base + 0, narrow.at[l, 15], row_in.at[1, 0, l], near["n"])
    copies.start(base + 1, narrow.at[l, 0], row_in.at[1, 1, l], near["s"])
    if l % 2 == 1:
        slot = 1 + l // 2
        edges[slot] = (picked_edges(narrow, pick, l - 1) + picked_edges(narrow, pick, l)).astype(BF16)
        copies.start(base + 2, edges.at[slot], edge_in.at[slot, 0], near["e"])
        copies.start(base + 3, edges.at[slot], edge_in.at[slot, 1], near["w"])


def second_step(copies, l, adv_ref, amount, middle, narrow, side, coef, band, row_in, edge_in):
    base = HALO_COPIES + 6 + 4 * l
    copies.arrived(base + 0, base + 1)
    if l % 2 == 0:
        copies.arrived(base + 6, base + 7)
    advance(middle, adv_ref, narrow, side, coef, band, row_in, edge_in, 1, l, False)


ADVECT_SCRATCH = [
    pltpu.VMEM((4, 18, SPECIES, 128), F32),
    pltpu.VMEM((4, 18, SPECIES, 128), F32),
    pltpu.VMEM((4, 16, SPECIES, 128), BF16),
    pltpu.VMEM((SPECIES, 128), BF16),
    pltpu.VMEM((8192, 128), BF16),
    pltpu.VMEM((3, SPECIES, 128), BF16),
    pltpu.VMEM((2, 2, 4, SPECIES, 128), BF16),
    pltpu.VMEM((3, 2, SPECIES, 128), BF16),
    pltpu.VMEM((2, 64, 128), F32),
    pltpu.VMEM((2, 64, 128), F32),
    pltpu.VMEM((4, 24, 128), F32),
    pltpu.VMEM((4, 3, 16, 128), F32),
    pltpu.VMEM((4, 16, 256, 128), BF16),
]
COPIES = HALO_COPIES + 22


def transport_kernel(met_hbm, weight_hbm, dest_ref, row_ref, tracer_ref, mx_ref, adv_ref, send, recv, load, fetch, met_ref, weight_ref, *scratch):
    cut = len(REGRID_SCRATCH)
    regrid_scratch = scratch[:cut]
    amount, middle, narrow, side, pick, edges, row_in, edge_in, courant, courant_in, shifted, coef, band = scratch[cut:]
    at, near = whereabouts(), neighbours()
    quarter = ITEMS // 4
    blocks = []
    for k in range(4):
        some = pl.ds(k * quarter, quarter)
        for which, (src, dst) in enumerate(((weight_hbm, weight_ref), (met_hbm, met_ref))):
            copy = pltpu.make_async_copy(src.at[some], dst.at[some], fetch.at[2 * k + which])
            copy.start()
            blocks.append(copy)
    barrier, count = greet(at, near)
    loads = start_tracers(tracer_ref, amount, load)
    for k in range(4):
        blocks[2 * k].wait()
        blocks[2 * k + 1].wait()
        contributions(met_ref, weight_ref, regrid_scratch[0], k)
    keys = keys_of(dest_ref[...], row_ref[...])
    pl.semaphore_wait(barrier, count)
    copies = Copies(send, recv)

    flow = Regrid(at, copies, keys, mx_ref, *regrid_scratch)
    every = range(3)
    for p in every:
        flow.open(p)

    edge_picker(pick)

    @pl.loop(0, 64)
    def _(k):
        band[k // 16, lax.rem(k, 16), 128:256, :] = jnp.zeros((128, 128), BF16)

    for p in every:
        flow.low_first(p)
        flow.low_second(p)
    for p in every:
        flow.high_first(p)
    first_rows(near, copies, loads, amount, narrow, row_in)
    first_columns(near, copies, narrow, pick, edges, edge_in)
    for p in every:
        flow.low_third(p)
    for p in every:
        flow.add_up(p, 0)
    for p in every:
        flow.high_rest(p)
    for p in every:
        flow.ring_on(p, 0)
    first_sends(near, copies, narrow, edges, row_in, edge_in)
    flow.add_up(0, 1)
    flow.ring_end(0, 0)
    flow.add_up(1, 1)
    flow.add_up(2, 1)
    for p in every:
        flow.ring_on(p, 1)
    flow.close(0, 0)
    send_courant(near, copies, mx_ref, courant, courant_in)
    flow.ring_end(1, 0)
    flow.ring_end(2, 0)
    coefficients(copies, courant, courant_in, shifted, coef, band)
    first = (amount, middle, narrow, side, pick, edges, coef, band, row_in, edge_in)
    second = (adv_ref, amount, middle, narrow, side, coef, band, row_in, edge_in)
    flow.ring_end(0, 1)
    first_step(near, copies, 0, *first)
    flow.ring_end(1, 1)
    flow.ring_end(2, 1)
    for l in range(1, 4):
        first_step(near, copies, l, *first)
    for l in range(4):
        second_step(copies, l, *second)
    flow.close(0, 1)
    light_of(mx_ref)
    for p in (1, 2):
        for half in range(2):
            flow.close(p, half)
    copies.sent()


def transport_call(met_src, weights, dest, row, tracers):
    vmem, anywhere = pl.BlockSpec(memory_space=pltpu.VMEM), pl.BlockSpec(memory_space=pl.ANY)
    dma = pltpu.SemaphoreType.DMA
    return pl.pallas_call(
        transport_kernel,
        out_shape=(pltpu.VMEM((1024, 128), F32), pltpu.VMEM((4, 16, SPECIES, 128), F32)),
        in_specs=[anywhere, anywhere, vmem, vmem, anywhere],
        out_specs=(vmem, vmem),
        scratch_shapes=[dma((COPIES,)), dma((COPIES,)), dma((64,)), dma((8,)), pltpu.VMEM(met_src.shape, BF16), pltpu.VMEM(weights.shape, BF16)] + REGRID_SCRATCH + ADVECT_SCRATCH,
        compiler_params=pltpu.CompilerParams(collective_id=0, has_side_effects=True, vmem_limit_bytes=54 << 20),
        name="transport",
    )(met_src, weights, dest, row, tracers)


CHUNK = 4


def thirds(value):
    first = value.astype(BF16)
    rest = value - first.astype(F32)
    second = rest.astype(BF16)
    return first, second, (rest - second.astype(F32)).astype(BF16)


def spread_rates(rate_in, photo_in, both, rates):
    nfields, count = rate_in.shape
    both[...] = jnp.zeros(both.shape, F32)
    both[0:nfields, 0:count] = rate_in[...]
    both[nfields : nfields + 1, 0:count] = photo_in[...]
    field, lane = lanes_of((16, 96), 0), lanes_of((16, 96), 1)
    total = jnp.zeros((SPECIES, 96), F32)
    for piece, (low, high) in zip(thirds(both[...].T), ((0, 48), (48, 80), (80, 96))):
        here = jnp.logical_and(jnp.logical_and(lane >= low, lane < high), lax.rem(lane, 16) == field)
        total = total + jnp.dot(piece, jnp.where(here, 1.0, 0.0).astype(BF16), preferred_element_type=F32)
    rates[...] = total.astype(BF16)


def chemistry_kernel(mx_ref, rate_in, photo_in, adv_ref, met_ref, out_ref, both, rates, result, store):
    chunks = 64 // CHUNK
    count = out_ref.shape[0]

    def put(lr):
        return pltpu.make_async_copy(result.at[lr, pl.ds(0, count)], out_ref.at[:, lr, 0], store.at[lr])

    met_ref[...] = mx_ref[0:768, :]
    spread_rates(rate_in, photo_in, both, rates)

    def fields(lr):
        value = mx_ref[pl.ds(lr, 16, stride=64), :]
        m1 = value.astype(BF16)
        rest = value - m1.astype(F32)
        m2 = rest.astype(BF16)
        m3 = (rest - m2.astype(F32)).astype(BF16)
        return jnp.concatenate([m1, m2, m3, m1, m2, m1], axis=0)

    @pl.loop(0, chunks)
    def _(k):
        for pair in range(CHUNK // 2):
            lr = k * CHUNK + 2 * pair
            rhs = jnp.concatenate([fields(lr), fields(lr + 1)], axis=1)
            exponent = jnp.dot(rates[...], rhs, preferred_element_type=F32)
            loss = jnp.maximum(exponent, 0.0) + jnp.log(1.0 + jnp.exp(-jnp.abs(exponent)))
            for side in range(2):
                result[lr + side] = adv_ref[lr + side] / (1.0 + loss[:, side * 128 : side * 128 + 128])
                put(lr + side).start()

    @pl.loop(0, 64)
    def _(lr):
        put(lr).wait()


def chemistry_call(mx, rate_coef, photo_coef, adv, count):
    vmem, anywhere = pl.BlockSpec(memory_space=pltpu.VMEM), pl.BlockSpec(memory_space=pl.ANY)
    dma = pltpu.SemaphoreType.DMA
    return pl.pallas_call(
        chemistry_kernel,
        out_shape=(jax.ShapeDtypeStruct((768, 128), F32), jax.ShapeDtypeStruct((count, 64, 1, 128), F32)),
        in_specs=[vmem] * 4,
        out_specs=(vmem, anywhere),
        scratch_shapes=[pltpu.VMEM((16, SPECIES), F32), pltpu.VMEM((SPECIES, 96), BF16), pltpu.VMEM((64, SPECIES, 128), F32), dma((64,))],
        compiler_params=pltpu.CompilerParams(vmem_limit_bytes=40 << 20),
        name="chemistry",
    )(mx, rate_coef, photo_coef, adv)


def local(met_src, intersection_weights, block_dest, block_row, tracers, rate_coef, photo_coef):
    species, levels, rows, cells = tracers.shape
    mx, adv = transport_call(met_src, intersection_weights, block_dest[None], block_row[None], tracers.reshape(species, levels * rows, 1, cells))
    met, out = chemistry_call(mx, rate_coef.T, photo_coef[None], adv.reshape(levels * rows, SPECIES, cells), species)
    return met.reshape(-1, levels, rows, cells), out.reshape(species, levels, rows, cells)


def solution(mesh):
    split = P(("face", "tile"))
    grid = P(None, None, "face", "tile")
    return jax.shard_map(
        local,
        mesh=mesh,
        in_specs=(split, split, split, split, grid, P(), P()),
        out_specs=(grid, grid),
        check_vma=False,
    )
```

```python
import functools
import jax
import jax.numpy as jnp
from jax import lax
from jax.experimental import pallas as pl
from jax.experimental.pallas import tpu as pltpu
from jax.sharding import PartitionSpec as P

MESH = pl.DeviceIdType.MESH
F32 = jnp.float32
BF16 = jnp.bfloat16
PARTS = (("x", "y", "z"), ("y", "z", "x"), ("z", "x", "y"))
RING = 4
ITEMS = 64
SLAB = 16 + 16 * ITEMS
CUT = 16 + 8 * ITEMS
PER_PART = 25


def whereabouts():
    face = lax.axis_index("face")
    tile = lax.axis_index("tile")
    return {"x": lax.rem(tile, 4), "y": face // 2, "z": tile // 4, "c": lax.rem(face, 2)}


def device(at):
    return (at["y"] * 2 + at["c"], at["z"] * 4 + at["x"])


def moved(at, dim, by):
    there = dict(at)
    there[dim] = 1 - at[dim] if dim == "c" else lax.rem(at[dim] + by, RING)
    return there


class Copies:
    def __init__(self, send, recv):
        self.send, self.recv, self.made, self.over = send, recv, {}, set()

    def start(self, index, src, dst, there):
        copy = pltpu.make_async_remote_copy(
            src_ref=src,
            dst_ref=dst,
            send_sem=self.send.at[index],
            recv_sem=self.recv.at[index],
            device_id=device(there) if isinstance(there, dict) else there,
            device_id_type=MESH,
        )
        copy.start()
        self.made[index] = copy

    def arrived(self, *indices):
        for index in indices:
            self.made[index].wait_recv()

    def sent_of(self, *indices):
        for index in indices:
            self.made[index].wait_send()
            self.over.add(index)

    def sent(self):
        self.sent_of(*[index for index in self.made if index not in self.over])


class Regrid:
    def __init__(self, at, copies, key_ref, mx_ref, cs, gath, mask, part_sum, relay, ring_in, full, cut_sum, last_in):
        self.at, self.copies, self.key_ref, self.mx_ref = at, copies, key_ref, mx_ref
        self.cs, self.gath, self.mask, self.part_sum, self.relay = cs, gath, mask, part_sum, relay
        self.ring_in, self.full, self.cut_sum, self.last_in = ring_in, full, cut_sum, last_in
        self.me = [at[dims[0]] * 2 + at["c"] for dims in PARTS]
        self.gather_rows = (pl.ds(0, CUT), pl.ds(CUT, SLAB - CUT))
        self.sum_rows = (pl.ds(0, 512), pl.ds(512, 512))

    def toward(self, p, k, by):
        return moved(self.at, PARTS[p][k], by)

    def arrived(self, p, *indices):
        self.copies.arrived(*[p * PER_PART + k for k in indices])

    def send(self, p, index, src, dst, there):
        self.copies.start(p * PER_PART + index, src, dst, there)

    def open(self, p):
        own, mate = self.gath.at[p, self.me[p]], moved(self.at, "c", 1)
        low, high = self.gather_rows
        self.gath[p, self.me[p], 0:16, :] = self.key_ref[p]
        self.gath[p, self.me[p], 16:SLAB, :] = self.cs[p * 1024 : (p + 1) * 1024, :].astype(BF16)
        self.send(p, 0, own.at[low], own.at[low], self.toward(p, 0, 1))
        self.send(p, 3, own.at[low], own.at[low], self.toward(p, 0, 3))
        self.send(p, 2, own.at[high], own.at[high], self.toward(p, 0, 3))
        self.send(p, 4, own, own, mate)

    def pass_on(self, p, half, step, index, there):
        slot = lax.rem(self.at[PARTS[p][0]] + step, RING) * 2 + self.at["c"]
        ref = self.gath.at[p, slot, self.gather_rows[half]]
        self.send(p, index, ref, ref, there)

    def low_first(self, p):
        mate, nxt = moved(self.at, "c", 1), self.toward(p, 0, 1)
        own, high = self.gath.at[p, self.me[p]], self.gather_rows[1]
        self.arrived(p, 0)
        self.pass_on(p, 0, 3, 5, nxt)
        self.send(p, 1, own.at[high], own.at[high], nxt)
        self.pass_on(p, 0, 3, 6, mate)

    def low_second(self, p):
        self.arrived(p, 3)
        self.pass_on(p, 0, 1, 10, moved(self.at, "c", 1))

    def high_first(self, p):
        mate, prv = moved(self.at, "c", 1), self.toward(p, 0, 3)
        self.arrived(p, 2)
        self.pass_on(p, 1, 1, 7, prv)
        self.pass_on(p, 1, 1, 8, mate)

    def low_third(self, p):
        self.arrived(p, 5)
        self.pass_on(p, 0, 2, 11, moved(self.at, "c", 1))

    def high_rest(self, p):
        mate = moved(self.at, "c", 1)
        self.arrived(p, 1)
        self.pass_on(p, 1, 3, 9, mate)
        self.arrived(p, 7)
        self.pass_on(p, 1, 2, 12, mate)

    def build_mask(self, p):
        gath, mask = self.gath, self.mask
        lane = lax.broadcasted_iota(jnp.int32, (1, 128), 1)
        rows = lax.broadcasted_iota(jnp.int32, (256, 128), 0).astype(F32)
        mine = self.me[p].astype(F32)
        for a in range(RING):
            k0 = gath[p, 2 * a, 0:16, :].astype(F32)
            k1 = gath[p, 2 * a + 1, 0:16, :].astype(F32)
            high_key = jnp.where(lane < ITEMS, k0[0:1, :], k1[0:1, :])
            low_key = jnp.where(lane < ITEMS, k0[8:9, :], k1[8:9, :])
            key = jnp.where(high_key == mine, low_key, -1.0)
            mask[p, :, a * 128 : (a + 1) * 128] = jnp.where(rows == key, 1.0, 0.0).astype(BF16)

    def add_up(self, p, half):
        gath, part_sum = self.gath, self.part_sum
        if half == 0:
            self.arrived(p, 4, 6, 10, 11)
            self.build_mask(p)
        else:
            self.arrived(p, 8, 9, 12)

        @pl.loop(0, 2)
        def _(twice):
            for inner in range(2):
                pair = half * 4 + twice * 2 + inner

                def level(fl):
                    start = pl.multiple_of(16 + fl * ITEMS, 16)
                    return jnp.concatenate([gath[p, s, pl.ds(start, ITEMS), :] for s in range(8)], axis=0)

                rhs = jnp.concatenate([level(2 * pair), level(2 * pair + 1)], axis=1)
                out = jnp.dot(self.mask[p], rhs, preferred_element_type=F32).astype(BF16)
                for side in range(2):
                    start = pl.multiple_of((2 * pair + side) * 64, 64)
                    for b in range(RING):
                        part_sum[p, b, pl.ds(start, 64), :] = out[b * 64 : (b + 1) * 64, side * 128 : (side + 1) * 128]

        nxt, prv = self.toward(p, 1, 1), self.toward(p, 1, 3)
        dim = PARTS[p][1]
        far, rows = lax.rem(self.at[dim] + 2, RING), self.sum_rows[half]
        if half == 0:
            self.send(p, 13, part_sum.at[p, far, rows], self.relay.at[p, 0], nxt)
            self.send(p, 16, part_sum.at[p, prv[dim], rows], self.ring_in.at[p, 1, rows], prv)
        else:
            self.send(p, 14, part_sum.at[p, far, rows], self.relay.at[p, 1], prv)
            self.send(p, 15, part_sum.at[p, nxt[dim], rows], self.ring_in.at[p, 0, rows], nxt)

    def ring_on(self, p, half):
        there = self.toward(p, 1, 3 if half else 1)
        to, rows = there[PARTS[p][1]], self.sum_rows[half]
        self.arrived(p, 13 + half)
        total = self.part_sum[p, to, rows, :].astype(F32) + self.relay[p, half].astype(F32)
        self.part_sum[p, to, rows, :] = total.astype(BF16)
        self.send(p, 17 + half, self.part_sum.at[p, to, rows], self.ring_in.at[p, half, rows], there)

    def ring_end(self, p, half):
        part_sum, ring_in, full, cut_sum = self.part_sum, self.ring_in, self.full, self.cut_sum
        if half == 0:
            self.arrived(p, 16, 17)
        else:
            self.arrived(p, 15, 18)
        own = self.at[PARTS[p][1]]

        @pl.loop(0, 4)
        def _(quad):
            for inner in range(2):
                fl = half * 8 + quad * 2 + inner
                block = pl.ds(pl.multiple_of(fl * 64, 64), 64)
                total = part_sum[p, own, block, :].astype(F32) + ring_in[p, 0, block, :].astype(F32) + ring_in[p, 1, block, :].astype(F32)
                full[p, block, :] = total
                narrow = total.astype(BF16)
                for c in range(RING):
                    cut_sum[p, c, pl.ds(pl.multiple_of(fl * 16, 16), 16), :] = narrow[c * 16 : (c + 1) * 16, :]

        rows = pl.ds(half * 128, 128)
        for k, by in enumerate((1, 3, 2)):
            there = self.toward(p, 2, by)
            self.send(p, 19 + half * 3 + k, cut_sum.at[p, there[PARTS[p][2]], rows], self.last_in.at[p, k, rows], there)

    def close(self, p, half):
        self.arrived(p, *[19 + half * 3 + k for k in range(3)])
        for fl in range(half * 8, half * 8 + 8):
            start = pl.multiple_of(fl * 64 + self.at[PARTS[p][2]] * 16, 16)
            here = slice(fl * 16, fl * 16 + 16)
            total = self.full[p, pl.ds(start, 16), :]
            for k in range(3):
                total = total + self.last_in[p, k, here, :].astype(F32)
            self.mx_ref[p * 256 + fl * 16 : p * 256 + fl * 16 + 16, :] = total


def contributions(met_ref, weight_ref, cs, part):
    @pl.loop(0, ITEMS // 16)
    def _(group):
        for k in range(4):
            s = part * (ITEMS // 4) + group * 4 + k
            cs[pl.ds(s, 48, stride=ITEMS), :] = jnp.dot(met_ref[s], weight_ref[s], preferred_element_type=F32)


def greet(at, near):
    barrier = pltpu.get_barrier_semaphore()
    peers = [moved(at, dim, by) for dim in ("x", "y", "z") for by in (1, 2, 3)] + [moved(at, "c", 1)]
    peers = [device(there) for there in peers] + [near[side] for side in "nsew"]
    for there in peers:
        pl.semaphore_signal(barrier, inc=1, device_id=there, device_id_type=MESH)
    return barrier, len(peers)


REGRID_SCRATCH = [
    pltpu.VMEM((48 * ITEMS, 128), F32),
    pltpu.VMEM((3, 8, SLAB, 128), BF16),
    pltpu.VMEM((3, 256, 512), BF16),
    pltpu.VMEM((3, RING, 1024, 128), BF16),
    pltpu.VMEM((3, 2, 512, 128), BF16),
    pltpu.VMEM((3, 2, 1024, 128), BF16),
    pltpu.VMEM((3, 1024, 128), F32),
    pltpu.VMEM((3, RING, 256, 128), BF16),
    pltpu.VMEM((3, 3, 256, 128), BF16),
]


def keys_of(dest, row):
    dest, row = jnp.concatenate([dest, dest], axis=1), jnp.concatenate([row, row], axis=1)
    face, tile = dest >> 4, dest & 15
    pos = {"x": tile & 3, "y": face >> 1, "z": tile >> 2}
    upper = lax.broadcasted_iota(jnp.int32, (16, 128), 0) < 8
    out = []
    for first, second, third in PARTS:
        high = pos[first] * 2 + (face & 1)
        low = pos[second] * 64 + pos[third] * 16 + row
        out.append(jnp.where(upper, high.astype(F32), low.astype(F32)).astype(BF16))
    return out


SPECIES = 256
UNROLL = 8
HALO_COPIES = 75


def lanes_of(shape, dim):
    return lax.broadcasted_iota(jnp.int32, shape, dim)


def edge_picker(pick):
    row, lane = lanes_of((128, 128), 0), lanes_of((128, 128), 1)

    @pl.loop(0, 64)
    def _(lr):
        east = jnp.logical_and(row == 127, lane == 2 * lr)
        west = jnp.logical_and(row == 0, lane == 2 * lr + 1)
        pick[pl.ds(pl.multiple_of(lr * 128, 128), 128), :] = jnp.where(jnp.logical_or(east, west), 1.0, 0.0).astype(BF16)


def picked_edges(narrow, pick, l):
    rows = jnp.concatenate([narrow[l, r] for r in range(16)], axis=1)
    start = l * 2048 if isinstance(l, int) else pl.multiple_of(l * 2048, 2048)
    return jnp.dot(rows, pick[pl.ds(start, 2048), :], preferred_element_type=F32)


def neighbours():
    face, tile = lax.axis_index("face"), lax.axis_index("tile")
    return {
        "n": (lax.rem(face + 1, 8), tile),
        "s": (lax.rem(face + 7, 8), tile),
        "e": (face, lax.rem(tile + 1, 16)),
        "w": (face, lax.rem(tile + 15, 16)),
    }


def start_tracers(tracer_ref, amount, load):
    count = tracer_ref.shape[0]
    copies = []
    for lr in range(64):
        copy = pltpu.make_async_copy(
            tracer_ref.at[:, lr, 0], amount.at[lr // 16, lr % 16 + 1, pl.ds(0, count)], load.at[lr]
        )
        copy.start()
        copies.append(copy)
    return copies


def first_rows(near, copies, loads, amount, narrow, row_in):
    for copy in loads:
        copy.wait()

    @pl.loop(0, 64)
    def _(lr):
        narrow[lr // 16, lax.rem(lr, 16)] = amount[lr // 16, lax.rem(lr, 16) + 1].astype(BF16)


def first_columns(near, copies, narrow, pick, edges, edge_in):
    edges[0] = lax.fori_loop(0, 4, lambda l, total: total + picked_edges(narrow, pick, l), jnp.zeros((SPECIES, 128), F32)).astype(BF16)


def first_sends(near, copies, narrow, edges, row_in, edge_in):
    copies.start(HALO_COPIES + 0, narrow.at[:, 15], row_in.at[0, 0], near["n"])
    copies.start(HALO_COPIES + 1, narrow.at[:, 0], row_in.at[0, 1], near["s"])
    copies.start(HALO_COPIES + 2, edges.at[0], edge_in.at[0, 0], near["e"])
    copies.start(HALO_COPIES + 3, edges.at[0], edge_in.at[0, 1], near["w"])


def send_courant(near, copies, mx_ref, courant, courant_in):
    courant[0] = 0.3 * jnp.tanh(mx_ref[0:64, :])
    courant[1] = 0.3 * jnp.tanh(mx_ref[64:128, :])
    copies.start(HALO_COPIES + 4, courant.at[0], courant_in.at[0], near["n"])
    copies.start(HALO_COPIES + 5, courant.at[1], courant_in.at[1], near["e"])


def light_of(mx_ref):
    depth = jnp.zeros((16, 128), F32)
    for l in range(4):
        value = mx_ref[128 + l * 16 : 144 + l * 16, :]
        depth = depth + (jnp.maximum(value, 0.0) + jnp.log1p(jnp.exp(-jnp.abs(value))))
        mx_ref[768 + l * 16 : 784 + l * 16, :] = jnp.exp(-depth)
    mx_ref[832:1024, :] = jnp.zeros((192, 128), F32)


def coefficients(copies, courant, courant_in, shifted, coef, band):
    row, lane = lanes_of((128, 128), 0), lanes_of((128, 128), 1)
    from_west = jnp.where(row == lane - 1, 1.0, 0.0)
    from_east = jnp.where(row == lane + 1, 1.0, 0.0)
    sub, edge = lanes_of((16, 128), 0), lanes_of((16, 128), 1)
    copies.arrived(HALO_COPIES + 4, HALO_COPIES + 5)
    for l in range(4):
        rows = slice(l * 16, l * 16 + 16)
        shifted[l, 8:24, :] = courant[0, rows, :]
        shifted[l, 7:8, :] = courant_in[0, l * 16 + 15 : l * 16 + 16, :]
        cx, cy = courant[0, rows, :], courant[1, rows, :]
        behind_x = shifted[l, 7:23, :]
        behind_y = jnp.where(edge == 0, pltpu.roll(courant_in[1, rows, :], 1, 1), pltpu.roll(cy, 1, 1))
        coef[l, 0] = 1.0 - jnp.maximum(cx, 0.0) + jnp.minimum(behind_x, 0.0) - jnp.maximum(cy, 0.0) + jnp.minimum(behind_y, 0.0)
        coef[l, 1] = jnp.maximum(behind_x, 0.0)
        coef[l, 2] = -jnp.minimum(cx, 0.0)
        west, east = jnp.maximum(behind_y, 0.0), -jnp.minimum(cy, 0.0)
        for r in range(16):
            w, e = west[r : r + 1, :], east[r : r + 1, :]
            band[l, r, 0:128, :] = (from_west * w + from_east * e).astype(BF16)
            lr = l * 16 + r
            k = 2 * lr % 16
            ends = jnp.where(jnp.logical_and(sub == k, edge == 0), w, jnp.where(jnp.logical_and(sub == k + 1, edge == 127), e, 0.0))
            band[l, r, 128 + 16 * (lr // 8) : 144 + 16 * (lr // 8), :] = ends.astype(BF16)


def advance(source, target, narrow, side, coef, band, row_in, edge_in, step, l, keep):
    source[l, 0] = row_in[step, 0, l].astype(F32)
    source[l, 17] = row_in[step, 1, l].astype(F32)
    even = lax.rem(lanes_of((SPECIES, 128), 1), 2) == 0
    if step == 0 and l == 0 or step == 1 and l % 2 == 0:
        slot = 0 if step == 0 else 1 + l // 2
        side[...] = jnp.where(even, edge_in[slot, 0].astype(F32), edge_in[slot, 1].astype(F32)).astype(BF16)

    @pl.loop(0, 16 // UNROLL)
    def _(group):
        across = []
        for k in range(UNROLL):
            r = group * UNROLL + k
            lhs = jnp.concatenate([narrow[l, r], side[...]], axis=1)
            across.append(jnp.dot(lhs, band[l, r], preferred_element_type=F32))
        for k in range(UNROLL):
            r = group * UNROLL + k
            total = coef[l, 0, pl.ds(r, 1), :] * source[l, r + 1] + coef[l, 1, pl.ds(r, 1), :] * source[l, r]
            total = total + coef[l, 2, pl.ds(r, 1), :] * source[l, r + 2] + across[k]
            target[l, r + keep] = total
            if keep:
                narrow[l, r] = total.astype(BF16)


def first_step(near, copies, l, amount, middle, narrow, side, pick, edges, coef, band, row_in, edge_in):
    if l == 0:
        copies.arrived(*[HALO_COPIES + k for k in range(4)])
        copies.sent_of(HALO_COPIES + 0, HALO_COPIES + 1)
    advance(amount, middle, narrow, side, coef, band, row_in, edge_in, 0, l, True)
    base = HALO_COPIES + 6 + 4 * l
    copies.start(base + 0, narrow.at[l, 15], row_in.at[1, 0, l], near["n"])
    copies.start(base + 1, narrow.at[l, 0], row_in.at[1, 1, l], near["s"])
    if l % 2 == 1:
        slot = 1 + l // 2
        edges[slot] = (picked_edges(narrow, pick, l - 1) + picked_edges(narrow, pick, l)).astype(BF16)
        copies.start(base + 2, edges.at[slot], edge_in.at[slot, 0], near["e"])
        copies.start(base + 3, edges.at[slot], edge_in.at[slot, 1], near["w"])


def second_step(copies, l, adv_ref, amount, middle, narrow, side, coef, band, row_in, edge_in):
    base = HALO_COPIES + 6 + 4 * l
    copies.arrived(base + 0, base + 1)
    if l % 2 == 0:
        copies.arrived(base + 6, base + 7)
    advance(middle, adv_ref, narrow, side, coef, band, row_in, edge_in, 1, l, False)


ADVECT_SCRATCH = [
    pltpu.VMEM((4, 18, SPECIES, 128), F32),
    pltpu.VMEM((4, 18, SPECIES, 128), F32),
    pltpu.VMEM((4, 16, SPECIES, 128), BF16),
    pltpu.VMEM((SPECIES, 128), BF16),
    pltpu.VMEM((8192, 128), BF16),
    pltpu.VMEM((3, SPECIES, 128), BF16),
    pltpu.VMEM((2, 2, 4, SPECIES, 128), BF16),
    pltpu.VMEM((3, 2, SPECIES, 128), BF16),
    pltpu.VMEM((2, 64, 128), F32),
    pltpu.VMEM((2, 64, 128), F32),
    pltpu.VMEM((4, 24, 128), F32),
    pltpu.VMEM((4, 3, 16, 128), F32),
    pltpu.VMEM((4, 16, 256, 128), BF16),
]
COPIES = HALO_COPIES + 22


def transport_kernel(met_hbm, weight_hbm, dest_ref, row_ref, tracer_ref, mx_ref, adv_ref, send, recv, load, fetch, met_ref, weight_ref, *scratch):
    cut = len(REGRID_SCRATCH)
    regrid_scratch = scratch[:cut]
    amount, middle, narrow, side, pick, edges, row_in, edge_in, courant, courant_in, shifted, coef, band = scratch[cut:]
    at, near = whereabouts(), neighbours()
    quarter = ITEMS // 4
    blocks = []
    for k in range(4):
        some = pl.ds(k * quarter, quarter)
        for which, (src, dst) in enumerate(((weight_hbm, weight_ref), (met_hbm, met_ref))):
            copy = pltpu.make_async_copy(src.at[some], dst.at[some], fetch.at[2 * k + which])
            copy.start()
            blocks.append(copy)
    barrier, count = greet(at, near)
    for k in range(4):
        blocks[2 * k].wait()
        blocks[2 * k + 1].wait()
        contributions(met_ref, weight_ref, regrid_scratch[0], k)
    keys = keys_of(dest_ref[...], row_ref[...])
    pl.semaphore_wait(barrier, count)
    copies = Copies(send, recv)

    flow = Regrid(at, copies, keys, mx_ref, *regrid_scratch)
    every = range(3)
    for p in every:
        flow.open(p)
    loads = start_tracers(tracer_ref, amount, load)

    edge_picker(pick)

    @pl.loop(0, 64)
    def _(k):
        band[k // 16, lax.rem(k, 16), 128:256, :] = jnp.zeros((128, 128), BF16)

    for p in every:
        flow.low_first(p)
        flow.low_second(p)
    for p in every:
        flow.high_first(p)
    first_rows(near, copies, loads, amount, narrow, row_in)
    first_columns(near, copies, narrow, pick, edges, edge_in)
    for p in every:
        flow.low_third(p)
    for p in every:
        flow.add_up(p, 0)
    for p in every:
        flow.high_rest(p)
    flow.add_up(0, 1)
    for p in every:
        flow.ring_on(p, 0)
    flow.add_up(1, 1)
    flow.add_up(2, 1)
    flow.ring_end(0, 0)
    first_sends(near, copies, narrow, edges, row_in, edge_in)
    for p in every:
        flow.ring_on(p, 1)
    flow.close(0, 0)
    send_courant(near, copies, mx_ref, courant, courant_in)
    flow.ring_end(1, 0)
    flow.ring_end(2, 0)
    coefficients(copies, courant, courant_in, shifted, coef, band)
    first = (amount, middle, narrow, side, pick, edges, coef, band, row_in, edge_in)
    second = (adv_ref, amount, middle, narrow, side, coef, band, row_in, edge_in)
    flow.ring_end(0, 1)
    first_step(near, copies, 0, *first)
    flow.ring_end(1, 1)
    flow.ring_end(2, 1)
    for l in range(1, 4):
        first_step(near, copies, l, *first)
    for l in range(4):
        second_step(copies, l, *second)
    flow.close(0, 1)
    light_of(mx_ref)
    for p in (1, 2):
        for half in range(2):
            flow.close(p, half)
    copies.sent()


def transport_call(met_src, weights, dest, row, tracers):
    vmem, anywhere = pl.BlockSpec(memory_space=pltpu.VMEM), pl.BlockSpec(memory_space=pl.ANY)
    dma = pltpu.SemaphoreType.DMA
    return pl.pallas_call(
        transport_kernel,
        out_shape=(pltpu.VMEM((1024, 128), F32), pltpu.VMEM((4, 16, SPECIES, 128), F32)),
        in_specs=[anywhere, anywhere, vmem, vmem, anywhere],
        out_specs=(vmem, vmem),
        scratch_shapes=[dma((COPIES,)), dma((COPIES,)), dma((64,)), dma((8,)), pltpu.VMEM(met_src.shape, BF16), pltpu.VMEM(weights.shape, BF16)] + REGRID_SCRATCH + ADVECT_SCRATCH,
        compiler_params=pltpu.CompilerParams(collective_id=0, has_side_effects=True, vmem_limit_bytes=54 << 20),
        name="transport",
    )(met_src, weights, dest, row, tracers)


CHUNK = 16


def thirds(value):
    first = value.astype(BF16)
    rest = value - first.astype(F32)
    second = rest.astype(BF16)
    return first, second, (rest - second.astype(F32)).astype(BF16)


def spread_rates(rate_in, photo_in, both, rates):
    nfields, count = rate_in.shape
    both[...] = jnp.zeros(both.shape, F32)
    both[0:nfields, 0:count] = rate_in[...]
    both[nfields : nfields + 1, 0:count] = photo_in[...]
    field, lane = lanes_of((16, 96), 0), lanes_of((16, 96), 1)
    total = jnp.zeros((SPECIES, 96), F32)
    for piece, (low, high) in zip(thirds(both[...].T), ((0, 48), (48, 80), (80, 96))):
        here = jnp.logical_and(jnp.logical_and(lane >= low, lane < high), lax.rem(lane, 16) == field)
        total = total + jnp.dot(piece, jnp.where(here, 1.0, 0.0).astype(BF16), preferred_element_type=F32)
    rates[...] = total.astype(BF16)


def chemistry_kernel(mx_ref, rate_in, photo_in, adv_ref, met_ref, out_ref, both, rates, result, store):
    chunks = 64 // CHUNK
    count = out_ref.shape[0]

    def put(lr):
        return pltpu.make_async_copy(result.at[lr, pl.ds(0, count)], out_ref.at[:, lr, 0], store.at[lr])

    met_ref[...] = mx_ref[0:768, :]
    spread_rates(rate_in, photo_in, both, rates)

    def fields(lr):
        value = mx_ref[pl.ds(lr, 16, stride=64), :]
        m1 = value.astype(BF16)
        rest = value - m1.astype(F32)
        m2 = rest.astype(BF16)
        m3 = (rest - m2.astype(F32)).astype(BF16)
        return jnp.concatenate([m1, m2, m3, m1, m2, m1], axis=0)

    @pl.loop(0, chunks)
    def _(k):
        for pair in range(CHUNK // 2):
            lr = k * CHUNK + 2 * pair
            rhs = jnp.concatenate([fields(lr), fields(lr + 1)], axis=1)
            exponent = jnp.dot(rates[...], rhs, preferred_element_type=F32)
            loss = jnp.maximum(exponent, 0.0) + jnp.log(1.0 + jnp.exp(-jnp.abs(exponent)))
            for side in range(2):
                result[lr + side] = adv_ref[lr + side] / (1.0 + loss[:, side * 128 : side * 128 + 128])
                put(lr + side).start()

    @pl.loop(0, 64)
    def _(lr):
        put(lr).wait()


def chemistry_call(mx, rate_coef, photo_coef, adv, count):
    vmem, anywhere = pl.BlockSpec(memory_space=pltpu.VMEM), pl.BlockSpec(memory_space=pl.ANY)
    dma = pltpu.SemaphoreType.DMA
    return pl.pallas_call(
        chemistry_kernel,
        out_shape=(jax.ShapeDtypeStruct((768, 128), F32), jax.ShapeDtypeStruct((count, 64, 1, 128), F32)),
        in_specs=[vmem] * 4,
        out_specs=(vmem, anywhere),
        scratch_shapes=[pltpu.VMEM((16, SPECIES), F32), pltpu.VMEM((SPECIES, 96), BF16), pltpu.VMEM((64, SPECIES, 128), F32), dma((64,))],
        compiler_params=pltpu.CompilerParams(vmem_limit_bytes=40 << 20),
        name="chemistry",
    )(mx, rate_coef, photo_coef, adv)


def local(met_src, intersection_weights, block_dest, block_row, tracers, rate_coef, photo_coef):
    species, levels, rows, cells = tracers.shape
    mx, adv = transport_call(met_src, intersection_weights, block_dest[None], block_row[None], tracers.reshape(species, levels * rows, 1, cells))
    met, out = chemistry_call(mx, rate_coef.T, photo_coef[None], adv.reshape(levels * rows, SPECIES, cells), species)
    return met.reshape(-1, levels, rows, cells), out.reshape(species, levels, rows, cells)


def solution(mesh):
    split = P(("face", "tile"))
    grid = P(None, None, "face", "tile")
    return jax.shard_map(
        local,
        mesh=mesh,
        in_specs=(split, split, split, split, grid, P(), P()),
        out_specs=(grid, grid),
        check_vma=False,
    )
```

```python
import functools
import jax
import jax.numpy as jnp
from jax import lax
from jax.experimental import pallas as pl
from jax.experimental.pallas import tpu as pltpu
from jax.sharding import PartitionSpec as P

MESH = pl.DeviceIdType.MESH
F32 = jnp.float32
BF16 = jnp.bfloat16
PARTS = (("x", "y", "z"), ("y", "z", "x"), ("z", "x", "y"))
RING = 4
ITEMS = 64
SLAB = 16 + 16 * ITEMS
CUT = 16 + 8 * ITEMS
PER_PART = 25


def whereabouts():
    face = lax.axis_index("face")
    tile = lax.axis_index("tile")
    return {"x": lax.rem(tile, 4), "y": face // 2, "z": tile // 4, "c": lax.rem(face, 2)}


def device(at):
    return (at["y"] * 2 + at["c"], at["z"] * 4 + at["x"])


def moved(at, dim, by):
    there = dict(at)
    there[dim] = 1 - at[dim] if dim == "c" else lax.rem(at[dim] + by, RING)
    return there


class Copies:
    def __init__(self, send, recv):
        self.send, self.recv, self.made, self.over = send, recv, {}, set()

    def start(self, index, src, dst, there):
        copy = pltpu.make_async_remote_copy(
            src_ref=src,
            dst_ref=dst,
            send_sem=self.send.at[index],
            recv_sem=self.recv.at[index],
            device_id=device(there) if isinstance(there, dict) else there,
            device_id_type=MESH,
        )
        copy.start()
        self.made[index] = copy

    def arrived(self, *indices):
        for index in indices:
            self.made[index].wait_recv()

    def sent_of(self, *indices):
        for index in indices:
            self.made[index].wait_send()
            self.over.add(index)

    def sent(self):
        self.sent_of(*[index for index in self.made if index not in self.over])


class Regrid:
    def __init__(self, at, copies, key_ref, mx_ref, cs, gath, mask, part_sum, relay, ring_in, full, cut_sum, last_in):
        self.at, self.copies, self.key_ref, self.mx_ref = at, copies, key_ref, mx_ref
        self.cs, self.gath, self.mask, self.part_sum, self.relay = cs, gath, mask, part_sum, relay
        self.ring_in, self.full, self.cut_sum, self.last_in = ring_in, full, cut_sum, last_in
        self.me = [at[dims[0]] * 2 + at["c"] for dims in PARTS]
        self.gather_rows = (pl.ds(0, CUT), pl.ds(CUT, SLAB - CUT))
        self.sum_rows = (pl.ds(0, 512), pl.ds(512, 512))

    def toward(self, p, k, by):
        return moved(self.at, PARTS[p][k], by)

    def arrived(self, p, *indices):
        self.copies.arrived(*[p * PER_PART + k for k in indices])

    def send(self, p, index, src, dst, there):
        self.copies.start(p * PER_PART + index, src, dst, there)

    def open(self, p):
        own, mate = self.gath.at[p, self.me[p]], moved(self.at, "c", 1)
        low, high = self.gather_rows
        self.gath[p, self.me[p], 0:16, :] = self.key_ref[p]
        self.gath[p, self.me[p], 16:SLAB, :] = self.cs[p * 1024 : (p + 1) * 1024, :].astype(BF16)
        self.send(p, 0, own.at[low], own.at[low], self.toward(p, 0, 1))
        self.send(p, 3, own.at[low], own.at[low], self.toward(p, 0, 3))
        self.send(p, 2, own.at[high], own.at[high], self.toward(p, 0, 3))
        self.send(p, 4, own, own, mate)

    def pass_on(self, p, half, step, index, there):
        slot = lax.rem(self.at[PARTS[p][0]] + step, RING) * 2 + self.at["c"]
        ref = self.gath.at[p, slot, self.gather_rows[half]]
        self.send(p, index, ref, ref, there)

    def low_first(self, p):
        mate, nxt = moved(self.at, "c", 1), self.toward(p, 0, 1)
        own, high = self.gath.at[p, self.me[p]], self.gather_rows[1]
        self.arrived(p, 0)
        self.pass_on(p, 0, 3, 5, nxt)
        self.send(p, 1, own.at[high], own.at[high], nxt)
        self.pass_on(p, 0, 3, 6, mate)

    def low_second(self, p):
        self.arrived(p, 3)
        self.pass_on(p, 0, 1, 10, moved(self.at, "c", 1))

    def high_first(self, p):
        mate, prv = moved(self.at, "c", 1), self.toward(p, 0, 3)
        self.arrived(p, 2)
        self.pass_on(p, 1, 1, 7, prv)
        self.pass_on(p, 1, 1, 8, mate)

    def low_third(self, p):
        self.arrived(p, 5)
        self.pass_on(p, 0, 2, 11, moved(self.at, "c", 1))

    def high_rest(self, p):
        mate = moved(self.at, "c", 1)
        self.arrived(p, 1)
        self.pass_on(p, 1, 3, 9, mate)
        self.arrived(p, 7)
        self.pass_on(p, 1, 2, 12, mate)

    def build_mask(self, p):
        gath, mask = self.gath, self.mask
        lane = lax.broadcasted_iota(jnp.int32, (1, 128), 1)
        rows = lax.broadcasted_iota(jnp.int32, (256, 128), 0).astype(F32)
        mine = self.me[p].astype(F32)
        for a in range(RING):
            k0 = gath[p, 2 * a, 0:16, :].astype(F32)
            k1 = gath[p, 2 * a + 1, 0:16, :].astype(F32)
            high_key = jnp.where(lane < ITEMS, k0[0:1, :], k1[0:1, :])
            low_key = jnp.where(lane < ITEMS, k0[8:9, :], k1[8:9, :])
            key = jnp.where(high_key == mine, low_key, -1.0)
            mask[p, :, a * 128 : (a + 1) * 128] = jnp.where(rows == key, 1.0, 0.0).astype(BF16)

    def add_up(self, p, half):
        gath, part_sum = self.gath, self.part_sum
        if half == 0:
            self.arrived(p, 4, 6, 10, 11)
            self.build_mask(p)
        else:
            self.arrived(p, 8, 9, 12)

        @pl.loop(0, 1)
        def _(twice):
            for inner in range(4):
                pair = half * 4 + twice * 4 + inner

                def level(fl):
                    start = pl.multiple_of(16 + fl * ITEMS, 16)
                    return jnp.concatenate([gath[p, s, pl.ds(start, ITEMS), :] for s in range(8)], axis=0)

                rhs = jnp.concatenate([level(2 * pair), level(2 * pair + 1)], axis=1)
                out = jnp.dot(self.mask[p], rhs, preferred_element_type=F32).astype(BF16)
                for side in range(2):
                    start = pl.multiple_of((2 * pair + side) * 64, 64)
                    for b in range(RING):
                        part_sum[p, b, pl.ds(start, 64), :] = out[b * 64 : (b + 1) * 64, side * 128 : (side + 1) * 128]

        nxt, prv = self.toward(p, 1, 1), self.toward(p, 1, 3)
        dim = PARTS[p][1]
        far, rows = lax.rem(self.at[dim] + 2, RING), self.sum_rows[half]
        if half == 0:
            self.send(p, 13, part_sum.at[p, far, rows], self.relay.at[p, 0], nxt)
            self.send(p, 16, part_sum.at[p, prv[dim], rows], self.ring_in.at[p, 1, rows], prv)
        else:
            self.send(p, 14, part_sum.at[p, far, rows], self.relay.at[p, 1], prv)
            self.send(p, 15, part_sum.at[p, nxt[dim], rows], self.ring_in.at[p, 0, rows], nxt)

    def ring_on(self, p, half):
        there = self.toward(p, 1, 3 if half else 1)
        to, rows = there[PARTS[p][1]], self.sum_rows[half]
        self.arrived(p, 13 + half)
        total = self.part_sum[p, to, rows, :].astype(F32) + self.relay[p, half].astype(F32)
        self.part_sum[p, to, rows, :] = total.astype(BF16)
        self.send(p, 17 + half, self.part_sum.at[p, to, rows], self.ring_in.at[p, half, rows], there)

    def ring_end(self, p, half):
        part_sum, ring_in, full, cut_sum = self.part_sum, self.ring_in, self.full, self.cut_sum
        if half == 0:
            self.arrived(p, 16, 17)
        else:
            self.arrived(p, 15, 18)
        own = self.at[PARTS[p][1]]

        @pl.loop(0, 4)
        def _(quad):
            for inner in range(2):
                fl = half * 8 + quad * 2 + inner
                block = pl.ds(pl.multiple_of(fl * 64, 64), 64)
                total = part_sum[p, own, block, :].astype(F32) + ring_in[p, 0, block, :].astype(F32) + ring_in[p, 1, block, :].astype(F32)
                full[p, block, :] = total
                narrow = total.astype(BF16)
                for c in range(RING):
                    cut_sum[p, c, pl.ds(pl.multiple_of(fl * 16, 16), 16), :] = narrow[c * 16 : (c + 1) * 16, :]

        rows = pl.ds(half * 128, 128)
        for k, by in enumerate((1, 3, 2)):
            there = self.toward(p, 2, by)
            self.send(p, 19 + half * 3 + k, cut_sum.at[p, there[PARTS[p][2]], rows], self.last_in.at[p, k, rows], there)

    def close(self, p, half):
        self.arrived(p, *[19 + half * 3 + k for k in range(3)])
        for fl in range(half * 8, half * 8 + 8):
            start = pl.multiple_of(fl * 64 + self.at[PARTS[p][2]] * 16, 16)
            here = slice(fl * 16, fl * 16 + 16)
            total = self.full[p, pl.ds(start, 16), :]
            for k in range(3):
                total = total + self.last_in[p, k, here, :].astype(F32)
            self.mx_ref[p * 256 + fl * 16 : p * 256 + fl * 16 + 16, :] = total


def contributions(met_ref, weight_ref, cs, part):
    @pl.loop(0, ITEMS // 16)
    def _(group):
        for k in range(4):
            s = part * (ITEMS // 4) + group * 4 + k
            cs[pl.ds(s, 48, stride=ITEMS), :] = jnp.dot(met_ref[s], weight_ref[s], preferred_element_type=F32)


def greet(at, near):
    barrier = pltpu.get_barrier_semaphore()
    peers = [moved(at, dim, by) for dim in ("x", "y", "z") for by in (1, 2, 3)] + [moved(at, "c", 1)]
    peers = [device(there) for there in peers] + [near[side] for side in "nsew"]
    for there in peers:
        pl.semaphore_signal(barrier, inc=1, device_id=there, device_id_type=MESH)
    return barrier, len(peers)


REGRID_SCRATCH = [
    pltpu.VMEM((48 * ITEMS, 128), F32),
    pltpu.VMEM((3, 8, SLAB, 128), BF16),
    pltpu.VMEM((3, 256, 512), BF16),
    pltpu.VMEM((3, RING, 1024, 128), BF16),
    pltpu.VMEM((3, 2, 512, 128), BF16),
    pltpu.VMEM((3, 2, 1024, 128), BF16),
    pltpu.VMEM((3, 1024, 128), F32),
    pltpu.VMEM((3, RING, 256, 128), BF16),
    pltpu.VMEM((3, 3, 256, 128), BF16),
]


def keys_of(dest, row):
    dest, row = jnp.concatenate([dest, dest], axis=1), jnp.concatenate([row, row], axis=1)
    face, tile = dest >> 4, dest & 15
    pos = {"x": tile & 3, "y": face >> 1, "z": tile >> 2}
    upper = lax.broadcasted_iota(jnp.int32, (16, 128), 0) < 8
    out = []
    for first, second, third in PARTS:
        high = pos[first] * 2 + (face & 1)
        low = pos[second] * 64 + pos[third] * 16 + row
        out.append(jnp.where(upper, high.astype(F32), low.astype(F32)).astype(BF16))
    return out


SPECIES = 256
UNROLL = 16
HALO_COPIES = 75


def lanes_of(shape, dim):
    return lax.broadcasted_iota(jnp.int32, shape, dim)


def edge_picker(pick):
    row, lane = lanes_of((128, 128), 0), lanes_of((128, 128), 1)

    @pl.loop(0, 64)
    def _(lr):
        east = jnp.logical_and(row == 127, lane == 2 * lr)
        west = jnp.logical_and(row == 0, lane == 2 * lr + 1)
        pick[pl.ds(pl.multiple_of(lr * 128, 128), 128), :] = jnp.where(jnp.logical_or(east, west), 1.0, 0.0).astype(BF16)


def picked_edges(narrow, pick, l):
    rows = jnp.concatenate([narrow[l, r] for r in range(16)], axis=1)
    start = l * 2048 if isinstance(l, int) else pl.multiple_of(l * 2048, 2048)
    return jnp.dot(rows, pick[pl.ds(start, 2048), :], preferred_element_type=F32)


def neighbours():
    face, tile = lax.axis_index("face"), lax.axis_index("tile")
    return {
        "n": (lax.rem(face + 1, 8), tile),
        "s": (lax.rem(face + 7, 8), tile),
        "e": (face, lax.rem(tile + 1, 16)),
        "w": (face, lax.rem(tile + 15, 16)),
    }


def start_tracers(tracer_ref, amount, load):
    count = tracer_ref.shape[0]
    copies = []
    for lr in range(64):
        copy = pltpu.make_async_copy(
            tracer_ref.at[:, lr, 0], amount.at[lr // 16, lr % 16 + 1, pl.ds(0, count)], load.at[lr]
        )
        copy.start()
        copies.append(copy)
    return copies


def first_rows(near, copies, loads, amount, narrow, row_in):
    for copy in loads:
        copy.wait()

    @pl.loop(0, 64)
    def _(lr):
        narrow[lr // 16, lax.rem(lr, 16)] = amount[lr // 16, lax.rem(lr, 16) + 1].astype(BF16)


def first_columns(near, copies, narrow, pick, edges, edge_in):
    edges[0] = lax.fori_loop(0, 4, lambda l, total: total + picked_edges(narrow, pick, l), jnp.zeros((SPECIES, 128), F32)).astype(BF16)


def first_sends(near, copies, narrow, edges, row_in, edge_in):
    copies.start(HALO_COPIES + 0, narrow.at[:, 15], row_in.at[0, 0], near["n"])
    copies.start(HALO_COPIES + 1, narrow.at[:, 0], row_in.at[0, 1], near["s"])
    copies.start(HALO_COPIES + 2, edges.at[0], edge_in.at[0, 0], near["e"])
    copies.start(HALO_COPIES + 3, edges.at[0], edge_in.at[0, 1], near["w"])


def send_courant(near, copies, mx_ref, courant, courant_in):
    courant[0] = 0.3 * jnp.tanh(mx_ref[0:64, :])
    courant[1] = 0.3 * jnp.tanh(mx_ref[64:128, :])
    copies.start(HALO_COPIES + 4, courant.at[0], courant_in.at[0], near["n"])
    copies.start(HALO_COPIES + 5, courant.at[1], courant_in.at[1], near["e"])


def light_of(mx_ref):
    depth = jnp.zeros((16, 128), F32)
    for l in range(4):
        value = mx_ref[128 + l * 16 : 144 + l * 16, :]
        depth = depth + (jnp.maximum(value, 0.0) + jnp.log1p(jnp.exp(-jnp.abs(value))))
        mx_ref[768 + l * 16 : 784 + l * 16, :] = jnp.exp(-depth)
    mx_ref[832:1024, :] = jnp.zeros((192, 128), F32)


def coefficients(copies, courant, courant_in, shifted, coef, band):
    row, lane = lanes_of((128, 128), 0), lanes_of((128, 128), 1)
    from_west = jnp.where(row == lane - 1, 1.0, 0.0)
    from_east = jnp.where(row == lane + 1, 1.0, 0.0)
    sub, edge = lanes_of((16, 128), 0), lanes_of((16, 128), 1)
    copies.arrived(HALO_COPIES + 4, HALO_COPIES + 5)
    for l in range(4):
        rows = slice(l * 16, l * 16 + 16)
        shifted[l, 8:24, :] = courant[0, rows, :]
        shifted[l, 7:8, :] = courant_in[0, l * 16 + 15 : l * 16 + 16, :]
        cx, cy = courant[0, rows, :], courant[1, rows, :]
        behind_x = shifted[l, 7:23, :]
        behind_y = jnp.where(edge == 0, pltpu.roll(courant_in[1, rows, :], 1, 1), pltpu.roll(cy, 1, 1))
        coef[l, 0] = 1.0 - jnp.maximum(cx, 0.0) + jnp.minimum(behind_x, 0.0) - jnp.maximum(cy, 0.0) + jnp.minimum(behind_y, 0.0)
        coef[l, 1] = jnp.maximum(behind_x, 0.0)
        coef[l, 2] = -jnp.minimum(cx, 0.0)
        west, east = jnp.maximum(behind_y, 0.0), -jnp.minimum(cy, 0.0)
        for r in range(16):
            w, e = west[r : r + 1, :], east[r : r + 1, :]
            band[l, r, 0:128, :] = (from_west * w + from_east * e).astype(BF16)
            lr = l * 16 + r
            k = 2 * lr % 16
            ends = jnp.where(jnp.logical_and(sub == k, edge == 0), w, jnp.where(jnp.logical_and(sub == k + 1, edge == 127), e, 0.0))
            band[l, r, 128 + 16 * (lr // 8) : 144 + 16 * (lr // 8), :] = ends.astype(BF16)


def advance(source, target, narrow, side, coef, band, row_in, edge_in, step, l, keep):
    source[l, 0] = row_in[step, 0, l].astype(F32)
    source[l, 17] = row_in[step, 1, l].astype(F32)
    even = lax.rem(lanes_of((SPECIES, 128), 1), 2) == 0
    if step == 0 and l == 0 or step == 1 and l % 2 == 0:
        slot = 0 if step == 0 else 1 + l // 2
        side[...] = jnp.where(even, edge_in[slot, 0].astype(F32), edge_in[slot, 1].astype(F32)).astype(BF16)

    @pl.loop(0, 16 // UNROLL)
    def _(group):
        across = []
        for k in range(UNROLL):
            r = group * UNROLL + k
            lhs = jnp.concatenate([narrow[l, r], side[...]], axis=1)
            across.append(jnp.dot(lhs, band[l, r], preferred_element_type=F32))
        for k in range(UNROLL):
            r = group * UNROLL + k
            total = coef[l, 0, pl.ds(r, 1), :] * source[l, r + 1] + coef[l, 1, pl.ds(r, 1), :] * source[l, r]
            total = total + coef[l, 2, pl.ds(r, 1), :] * source[l, r + 2] + across[k]
            target[l, r + keep] = total
            if keep:
                narrow[l, r] = total.astype(BF16)


def first_step(near, copies, l, amount, middle, narrow, side, pick, edges, coef, band, row_in, edge_in):
    if l == 0:
        copies.arrived(*[HALO_COPIES + k for k in range(4)])
        copies.sent_of(HALO_COPIES + 0, HALO_COPIES + 1)
    advance(amount, middle, narrow, side, coef, band, row_in, edge_in, 0, l, True)
    base = HALO_COPIES + 6 + 4 * l
    copies.start(base + 0, narrow.at[l, 15], row_in.at[1, 0, l], near["n"])
    copies.start(base + 1, narrow.at[l, 0], row_in.at[1, 1, l], near["s"])
    if l % 2 == 1:
        slot = 1 + l // 2
        edges[slot] = (picked_edges(narrow, pick, l - 1) + picked_edges(narrow, pick, l)).astype(BF16)
        copies.start(base + 2, edges.at[slot], edge_in.at[slot, 0], near["e"])
        copies.start(base + 3, edges.at[slot], edge_in.at[slot, 1], near["w"])


def second_step(copies, l, adv_ref, amount, middle, narrow, side, coef, band, row_in, edge_in):
    base = HALO_COPIES + 6 + 4 * l
    copies.arrived(base + 0, base + 1)
    if l % 2 == 0:
        copies.arrived(base + 6, base + 7)
    advance(middle, adv_ref, narrow, side, coef, band, row_in, edge_in, 1, l, False)


ADVECT_SCRATCH = [
    pltpu.VMEM((4, 18, SPECIES, 128), F32),
    pltpu.VMEM((4, 18, SPECIES, 128), F32),
    pltpu.VMEM((4, 16, SPECIES, 128), BF16),
    pltpu.VMEM((SPECIES, 128), BF16),
    pltpu.VMEM((8192, 128), BF16),
    pltpu.VMEM((3, SPECIES, 128), BF16),
    pltpu.VMEM((2, 2, 4, SPECIES, 128), BF16),
    pltpu.VMEM((3, 2, SPECIES, 128), BF16),
    pltpu.VMEM((2, 64, 128), F32),
    pltpu.VMEM((2, 64, 128), F32),
    pltpu.VMEM((4, 24, 128), F32),
    pltpu.VMEM((4, 3, 16, 128), F32),
    pltpu.VMEM((4, 16, 256, 128), BF16),
]
COPIES = HALO_COPIES + 22


def transport_kernel(met_hbm, weight_hbm, dest_ref, row_ref, tracer_ref, mx_ref, adv_ref, send, recv, load, fetch, met_ref, weight_ref, *scratch):
    cut = len(REGRID_SCRATCH)
    regrid_scratch = scratch[:cut]
    amount, middle, narrow, side, pick, edges, row_in, edge_in, courant, courant_in, shifted, coef, band = scratch[cut:]
    at, near = whereabouts(), neighbours()
    quarter = ITEMS // 4
    blocks = []
    for k in range(4):
        some = pl.ds(k * quarter, quarter)
        for which, (src, dst) in enumerate(((weight_hbm, weight_ref), (met_hbm, met_ref))):
            copy = pltpu.make_async_copy(src.at[some], dst.at[some], fetch.at[2 * k + which])
            copy.start()
            blocks.append(copy)
    barrier, count = greet(at, near)
    for k in range(4):
        blocks[2 * k].wait()
        blocks[2 * k + 1].wait()
        contributions(met_ref, weight_ref, regrid_scratch[0], k)
    keys = keys_of(dest_ref[...], row_ref[...])
    pl.semaphore_wait(barrier, count)
    copies = Copies(send, recv)

    flow = Regrid(at, copies, keys, mx_ref, *regrid_scratch)
    every = range(3)
    for p in every:
        flow.open(p)
    loads = start_tracers(tracer_ref, amount, load)

    edge_picker(pick)

    @pl.loop(0, 64)
    def _(k):
        band[k // 16, lax.rem(k, 16), 128:256, :] = jnp.zeros((128, 128), BF16)

    for p in every:
        flow.low_first(p)
        flow.low_second(p)
    for p in every:
        flow.high_first(p)
    first_rows(near, copies, loads, amount, narrow, row_in)
    first_columns(near, copies, narrow, pick, edges, edge_in)
    for p in every:
        flow.low_third(p)
    for p in every:
        flow.add_up(p, 0)
    for p in every:
        flow.high_rest(p)
    flow.add_up(0, 1)
    for p in every:
        flow.ring_on(p, 0)
    flow.add_up(1, 1)
    flow.add_up(2, 1)
    flow.ring_end(0, 0)
    first_sends(near, copies, narrow, edges, row_in, edge_in)
    for p in every:
        flow.ring_on(p, 1)
    flow.close(0, 0)
    send_courant(near, copies, mx_ref, courant, courant_in)
    flow.ring_end(1, 0)
    flow.ring_end(2, 0)
    coefficients(copies, courant, courant_in, shifted, coef, band)
    first = (amount, middle, narrow, side, pick, edges, coef, band, row_in, edge_in)
    second = (adv_ref, amount, middle, narrow, side, coef, band, row_in, edge_in)
    flow.ring_end(0, 1)
    first_step(near, copies, 0, *first)
    flow.ring_end(1, 1)
    flow.ring_end(2, 1)
    for l in range(1, 4):
        first_step(near, copies, l, *first)
    for l in range(4):
        second_step(copies, l, *second)
    flow.close(0, 1)
    light_of(mx_ref)
    for p in (1, 2):
        for half in range(2):
            flow.close(p, half)
    copies.sent()


def transport_call(met_src, weights, dest, row, tracers):
    vmem, anywhere = pl.BlockSpec(memory_space=pltpu.VMEM), pl.BlockSpec(memory_space=pl.ANY)
    dma = pltpu.SemaphoreType.DMA
    return pl.pallas_call(
        transport_kernel,
        out_shape=(pltpu.VMEM((1024, 128), F32), pltpu.VMEM((4, 16, SPECIES, 128), F32)),
        in_specs=[anywhere, anywhere, vmem, vmem, anywhere],
        out_specs=(vmem, vmem),
        scratch_shapes=[dma((COPIES,)), dma((COPIES,)), dma((64,)), dma((8,)), pltpu.VMEM(met_src.shape, BF16), pltpu.VMEM(weights.shape, BF16)] + REGRID_SCRATCH + ADVECT_SCRATCH,
        compiler_params=pltpu.CompilerParams(collective_id=0, has_side_effects=True, vmem_limit_bytes=54 << 20),
        name="transport",
    )(met_src, weights, dest, row, tracers)


CHUNK = 32


def thirds(value):
    first = value.astype(BF16)
    rest = value - first.astype(F32)
    second = rest.astype(BF16)
    return first, second, (rest - second.astype(F32)).astype(BF16)


def spread_rates(rate_in, photo_in, both, rates):
    nfields, count = rate_in.shape
    both[...] = jnp.zeros(both.shape, F32)
    both[0:nfields, 0:count] = rate_in[...]
    both[nfields : nfields + 1, 0:count] = photo_in[...]
    field, lane = lanes_of((16, 96), 0), lanes_of((16, 96), 1)
    total = jnp.zeros((SPECIES, 96), F32)
    for piece, (low, high) in zip(thirds(both[...].T), ((0, 48), (48, 80), (80, 96))):
        here = jnp.logical_and(jnp.logical_and(lane >= low, lane < high), lax.rem(lane, 16) == field)
        total = total + jnp.dot(piece, jnp.where(here, 1.0, 0.0).astype(BF16), preferred_element_type=F32)
    rates[...] = total.astype(BF16)


def chemistry_kernel(mx_ref, rate_in, photo_in, adv_ref, met_ref, out_ref, both, rates, result, store):
    chunks = 64 // CHUNK
    count = out_ref.shape[0]

    def put(lr):
        return pltpu.make_async_copy(result.at[lr, pl.ds(0, count)], out_ref.at[:, lr, 0], store.at[lr])

    met_ref[...] = mx_ref[0:768, :]
    spread_rates(rate_in, photo_in, both, rates)

    def fields(lr):
        value = mx_ref[pl.ds(lr, 16, stride=64), :]
        m1 = value.astype(BF16)
        rest = value - m1.astype(F32)
        m2 = rest.astype(BF16)
        m3 = (rest - m2.astype(F32)).astype(BF16)
        return jnp.concatenate([m1, m2, m3, m1, m2, m1], axis=0)

    @pl.loop(0, chunks)
    def _(k):
        for pair in range(CHUNK // 2):
            lr = k * CHUNK + 2 * pair
            rhs = jnp.concatenate([fields(lr), fields(lr + 1)], axis=1)
            exponent = jnp.dot(rates[...], rhs, preferred_element_type=F32)
            loss = jnp.maximum(exponent, 0.0) + jnp.log(1.0 + jnp.exp(-jnp.abs(exponent)))
            for side in range(2):
                result[lr + side] = adv_ref[lr + side] / (1.0 + loss[:, side * 128 : side * 128 + 128])
                put(lr + side).start()

    @pl.loop(0, 64)
    def _(lr):
        put(lr).wait()


def chemistry_call(mx, rate_coef, photo_coef, adv, count):
    vmem, anywhere = pl.BlockSpec(memory_space=pltpu.VMEM), pl.BlockSpec(memory_space=pl.ANY)
    dma = pltpu.SemaphoreType.DMA
    return pl.pallas_call(
        chemistry_kernel,
        out_shape=(jax.ShapeDtypeStruct((768, 128), F32), jax.ShapeDtypeStruct((count, 64, 1, 128), F32)),
        in_specs=[vmem] * 4,
        out_specs=(vmem, anywhere),
        scratch_shapes=[pltpu.VMEM((16, SPECIES), F32), pltpu.VMEM((SPECIES, 96), BF16), pltpu.VMEM((64, SPECIES, 128), F32), dma((64,))],
        compiler_params=pltpu.CompilerParams(vmem_limit_bytes=40 << 20),
        name="chemistry",
    )(mx, rate_coef, photo_coef, adv)


def local(met_src, intersection_weights, block_dest, block_row, tracers, rate_coef, photo_coef):
    species, levels, rows, cells = tracers.shape
    mx, adv = transport_call(met_src, intersection_weights, block_dest[None], block_row[None], tracers.reshape(species, levels * rows, 1, cells))
    met, out = chemistry_call(mx, rate_coef.T, photo_coef[None], adv.reshape(levels * rows, SPECIES, cells), species)
    return met.reshape(-1, levels, rows, cells), out.reshape(species, levels, rows, cells)


def solution(mesh):
    split = P(("face", "tile"))
    grid = P(None, None, "face", "tile")
    return jax.shard_map(
        local,
        mesh=mesh,
        in_specs=(split, split, split, split, grid, P(), P()),
        out_specs=(grid, grid),
        check_vma=False,
    )
```
